32 devices in a mesh: batch: 8 (over z, core), head: 4 (over y, x).
Axes of the slice: x: 2, y: 2, z: 4, core: 2. Of those that a mesh axis runs over, the one named last changes fastest.
Arguments:
- hidden_in: bfloat16 [2048, 2048], P(('batch', 'head')), may hold values from -6 to 6
- norm1_gain: float32 [2048], replicated, may hold values from 0.5 to 1.5
- qkv_weight: bfloat16 [3, 2048, 2048], P(None, None, 'head'), may hold values from -0.125 to 0.125
- beta_weight: bfloat16 [2048, 16], P(None, 'head'), may hold values from -0.125 to 0.125
- conv_weight: bfloat16 [3, 4, 2048], P(None, None, 'head'), may hold values from -3 to 3
- out_gain: float32 [128], replicated, may hold values from 0.5 to 1.5
- out_weight: bfloat16 [2048, 2048], P('head'), may hold values from -0.125 to 0.125
- norm2_gain: float32 [2048], replicated, may hold values from 0.5 to 1.5
- gate_up_weight: bfloat16 [2, 2048, 5632], P(None, None, 'head'), may hold values from -0.125 to 0.125
- down_weight: bfloat16 [5632, 2048], P('head'), may hold values from -0.078125 to 0.078125
- block_segments: int32 [8, 4], P('batch'), may hold values from 0 to 2, never falling along the last dimension, each value on 1 to 2 neighbouring positions
- cotangent: bfloat16 [2048, 2048], P(('batch', 'head')), may hold values from -6 to 6
Outputs:
- block_out: bfloat16 [2048, 2048], P(('batch', 'head'))
- input_grad: float32 [2048, 2048], P(('batch', 'head'))
- norm1_gain_grad: float32 [2048], replicated
- qkv_grad: float32 [3, 2048, 2048], P(None, None, 'head')
- beta_grad: float32 [2048, 16], P(None, 'head')
- conv_grad: float32 [3, 4, 2048], P(None, None, 'head')
- out_gain_grad: float32 [128], replicated
- out_grad: float32 [2048, 2048], P('head')
- norm2_gain_grad: float32 [2048], replicated
- gate_up_grad: float32 [2, 2048, 5632], P(None, None, 'head')
- down_grad: float32 [5632, 2048], P('head')
The draws below stay inside these ranges and needn't reach their ends.
Inputs may be any that keep to these rules, and one draw needn't show every extreme that they name: `block_segments`: each row gives, for each block of 64 tokens of one group in order, the number of the sequence it belongs to: three sequences in every group, numbered from 0 and never falling; each covers 1 to 2 blocks and one covers exactly 2.
All inputs are finite; a program needn't handle non-finite values.
Results may differ from the reference program's by a relative error of at most 0.02.
Values may be sent and summed in bfloat16 or wider, within the bound.
No kernel may reach another device: no remote copies, remote signals or barrier semaphores. Data moves between devices by JAX's collectives and lax.ppermute only.
A program may use at most 256 MiB of HBM per device.

```python
import math
import jax
import jax.numpy as jnp
import numpy as np
from jax import lax

D = 2048
HEADS = 16
HEAD_DIM = 128
FF = 5632
CONV = 4
BLOCK = 64
GROUP_TOK = 256
GROUPS = 8
TOKENS = 2048
BLOCKS = 4


def block_scale(key, dims, shards, low, high):
    factor_of, own = 1.0, jax.random.fold_in(key, 6)
    for position, blocks in shards:
        steps = jnp.exp(jax.random.uniform(jax.random.fold_in(own, position), (blocks,), jnp.float32, low / len(shards), high / len(shards)))
        factor_of = factor_of * jnp.repeat(steps, dims[position] // blocks).reshape([-1 if axis == position else 1 for axis in range(len(dims))])
    return factor_of


def split_up(amount, total, reach, skew):
    weights = [(1 << 20) // math.isqrt(standing ** skew) + 1 for standing in range(2, amount + 1)]
    spare, counts = total - reach - (amount - 1), [1] * (amount - 1)
    while spare > 0:
        movable = [i for i in range(amount - 1) if counts[i] < reach]
        whole, left = sum([weights[i] for i in movable]), spare
        for i in movable:
            more = min(reach - counts[i], max(1, left * weights[i] // whole), spare)
            counts[i] = counts[i] + more
            spare = spare - more
    return np.array([reach] + counts)


def uneven(own_key, number_of, total, bound, slope):
    if number_of == 2:
        one = jax.random.randint(own_key, (), max(1, total - bound), min(bound, total - 1) + 1)
        return jnp.stack([one, total - one])
    tallies = jnp.asarray(split_up(number_of, total, bound, slope), jnp.int32)
    pairs = (number_of - 1) // 2
    giver, receiver = tallies[1:1 + 2 * pairs:2], tallies[2:2 + 2 * pairs:2]
    slack = jnp.minimum(giver - 1, bound - receiver)
    shifted = jax.random.randint(jax.random.fold_in(own_key, 1), (pairs,), 0, 1 << 20) % (slack + 1)
    tallies = tallies.at[1:1 + 2 * pairs:2].set(giver - shifted).at[2:2 + 2 * pairs:2].set(receiver + shifted)
    return tallies[jax.random.permutation(jax.random.fold_in(own_key, 2), number_of)]


def centred(own_key, extent, scale, bound, cuts=(), held_as=jnp.bfloat16):
    factor_of = block_scale(own_key, extent, cuts, -0.22, 0.18) if cuts else 1.0
    values = jax.random.normal(own_key, extent, jnp.float32) * scale * factor_of
    return jnp.minimum(jnp.maximum(values, -bound), bound).astype(held_as)


def setup_inputs(seed: int = 0) -> dict:
    splits = jax.random.split(jax.random.key(seed), 13)
    return {
        "hidden_in": centred(splits[0], (TOKENS, D), 1.0, 6.0, ((0, 32),)),
        "norm1_gain": jnp.clip(1.0 + 0.1 * jax.random.normal(splits[1], (D,), jnp.float32), 0.5, 1.5),
        "qkv_weight": centred(splits[2], (3, D, D), D ** -0.5, 0.125, ((2, 4),)),
        "beta_weight": centred(splits[3], (D, HEADS), D ** -0.5, 0.125, ((1, 4),)),
        "conv_weight": centred(splits[4], (3, CONV, D), CONV ** -0.5, 3.0, ((2, 4),)),
        "out_gain": jnp.clip(1.0 + 0.1 * jax.random.normal(splits[5], (HEAD_DIM,), jnp.float32), 0.5, 1.5),
        "out_weight": centred(splits[6], (D, D), D ** -0.5, 0.125, ((0, 4),)),
        "norm2_gain": jnp.clip(1.0 + 0.1 * jax.random.normal(splits[7], (D,), jnp.float32), 0.5, 1.5),
        "gate_up_weight": centred(splits[8], (2, D, FF), D ** -0.5, 0.125, ((2, 4),)),
        "down_weight": centred(splits[9], (FF, D), FF ** -0.5, 0.078125, ((0, 4),)),
        "block_segments": jax.vmap(lambda own: jnp.searchsorted(jnp.cumsum(uneven(own, 3, BLOCKS, BLOCKS // 2, 2)), jnp.arange(BLOCKS), side="right"))(jax.random.split(splits[10], GROUPS)).reshape((GROUPS, BLOCKS)).astype(jnp.int32),
        "cotangent": centred(splits[11], (TOKENS, D), 1.0, 6.0, ((0, 32),)),
    }


highest_precision = lax.Precision.HIGHEST

@jax.custom_vjp
def low(v):
    return lax.optimization_barrier(v.astype(jnp.bfloat16)).astype(jnp.float32)

@jax.custom_vjp
def low_back(v):
    return v

def low_keep(v):
    return (low(v), None)

def low_pass(kept, grad):
    return (grad,)

def back_keep(v):
    return (v, None)

def back_low(kept, grad):
    return (low(grad),)
low.defvjp(low_keep, low_pass)
low_back.defvjp(back_keep, back_low)

def rms_norm(values, gain, epsilon):
    return values * lax.rsqrt(lax.optimization_barrier(jnp.mean(values * values, axis=-1, keepdims=True)) + epsilon) * gain

def unit_rows(field):
    return field * lax.rsqrt(lax.optimization_barrier(jnp.sum(field * field, axis=-1, keepdims=True)) + 1e-06)

def conv_masks(token_segments, taps):
    masks = []
    for shift in range(1, taps):
        earlier = jnp.concatenate([jnp.full((shift,), -1, jnp.int32), token_segments[:-shift].astype(jnp.int32)])
        masks.append((earlier == token_segments.astype(jnp.int32)).astype(jnp.float32)[:, None])
    return masks

def short_conv(values, taps, masks):
    result = values * taps[0]
    for shift in range(1, taps.shape[0]):
        moved = jnp.concatenate([jnp.zeros((shift, values.shape[1]), jnp.float32), values[:-shift]], axis=0)
        result = result + moved * taps[shift] * masks[shift - 1]
    return result

def block_step(running_state, inputs):
    query_rows, key, value, beta, keep = inputs
    running_state = running_state * keep
    length = key.shape[1]
    strict = jnp.tril(jnp.ones((length, length), jnp.float32), -1)
    inclusive = jnp.tril(jnp.ones((length, length), jnp.float32))
    keyed = jnp.einsum('hck,hdk->hcd', key * beta[:, :, None], key, precision=highest_precision) * strict
    power = -keyed
    inverse = jnp.eye(length, dtype=jnp.float32) + power
    for level in range(length.bit_length() - 2):
        power = jnp.einsum('hcd,hde->hce', power, power, precision=highest_precision)
        inverse = inverse + jnp.einsum('hcd,hde->hce', inverse, power, precision=highest_precision)
    weights = inverse * beta[:, None, :]
    weighted_key = jnp.einsum('hcd,hdk->hck', weights, key, precision=highest_precision)
    weighted_value = jnp.einsum('kzw,kwp->kzp', weights, value, precision=highest_precision)
    fresh_values = weighted_value - jnp.einsum('imd,ide->ime', weighted_key, running_state, precision=highest_precision)
    score_matrix = jnp.einsum('hck,hdk->hcd', query_rows, key, precision=highest_precision) * inclusive
    output_rows = jnp.einsum('imd,ide->ime', query_rows, running_state, precision=highest_precision) + jnp.einsum('kzw,kwp->kzp', score_matrix, fresh_values, precision=highest_precision)
    running_state = running_state + jnp.einsum('sbi,sbw->siw', key, fresh_values, precision=highest_precision)
    return (running_state, output_rows)

def local_mixer(projected, beta_logit, conv_taps, gain, token_segments, keep):
    masks = conv_masks(token_segments, conv_taps.shape[1])
    heads = beta_logit.shape[1]
    length = projected.shape[1]
    width = projected.shape[2] // heads
    blocks = keep.shape[0]
    size = length // blocks
    parts = []
    for which in range(3):
        convolved = jax.nn.silu(short_conv(projected[which], conv_taps[which], masks))
        parts.append(convolved.reshape(length, heads, width))
    query_rows = unit_rows(parts[0]) * width ** (-0.5)
    key = unit_rows(parts[1])
    value = parts[2]
    beta = jax.nn.sigmoid(beta_logit)

    def arrange(field):
        return field.reshape(blocks, size, heads, width).transpose(0, 2, 1, 3)
    beta_blocks = beta.reshape(blocks, size, heads).transpose(0, 2, 1)
    initial = jnp.zeros((heads, width, width), jnp.float32)
    final, outputs = lax.scan(jax.checkpoint(block_step), initial, (arrange(query_rows), arrange(key), arrange(value), beta_blocks, keep))
    outputs = outputs.transpose(0, 2, 1, 3).reshape(length, heads, width)
    return rms_norm(outputs, gain, 1e-05).reshape(length, heads * width)

def group_forward(params, values, token_segments, keep):
    norm1_gain, qkv_w, beta_w, conv_w, out_gain, out_w, norm2_gain, gate_up_w, down_w = params
    normed = low(rms_norm(values, norm1_gain, 1e-06))
    projected = low_back(jnp.einsum('td,sde->ste', normed, qkv_w, precision=highest_precision))
    beta_logit = low_back(jnp.dot(normed, beta_w, precision=highest_precision))
    mixed = low(local_mixer(projected, beta_logit, conv_w, out_gain, token_segments, keep))
    attn = low_back(jnp.dot(mixed, out_w, precision=highest_precision))
    middle = values + attn
    second = low(rms_norm(middle, norm2_gain, 1e-06))
    gate_up = low_back(jnp.einsum('td,sdf->stf', second, gate_up_w, precision=highest_precision))
    hidden = low(jax.nn.silu(gate_up[0]) * gate_up[1])
    return middle + jnp.dot(hidden, down_w, precision=highest_precision)

def add_pair(first, second):
    return first + second

def reference(hidden_in, norm1_gain, qkv_weight, beta_weight, conv_weight, out_gain, out_weight, norm2_gain, gate_up_weight, down_weight, block_segments, cotangent):
    params = tuple((item.astype(jnp.float32) for item in (norm1_gain, qkv_weight, beta_weight, conv_weight, out_gain, out_weight, norm2_gain, gate_up_weight, down_weight)))
    rows_all = hidden_in.astype(jnp.float32).reshape(GROUPS, GROUP_TOK, D)
    cot_all = cotangent.astype(jnp.float32).reshape(GROUPS, GROUP_TOK, D)

    def per_group(totals, group_data):
        values, incoming, segments = group_data
        token_segments = jnp.repeat(segments.astype(jnp.int32), BLOCK)
        keep = jnp.concatenate([jnp.zeros((1,), jnp.float32), (segments[1:] == segments[:-1]).astype(jnp.float32)])

        def forward(weights, values_in):
            return group_forward(weights, values_in, token_segments, keep)
        result, pullback = jax.vjp(forward, params, values)
        weight_grads, values_grad = pullback(incoming)
        totals = jax.tree.map(add_pair, totals, weight_grads)
        return (totals, (result.astype(jnp.bfloat16), values_grad))
    initial = jax.tree.map(jnp.zeros_like, params)
    totals, results = lax.scan(per_group, initial, (rows_all, cot_all, block_segments))
    outputs, grads = results
    return (outputs.reshape(TOKENS, D), grads.reshape(TOKENS, D), totals[0], totals[1], totals[2], totals[3], totals[4], totals[5], totals[6], totals[7], totals[8])
```

```python
import jax
import jax.numpy as jnp
from jax import lax
from jax.sharding import Mesh, PartitionSpec as P

highest_precision = lax.Precision.HIGHEST
f32 = jnp.float32
bf16 = jnp.bfloat16


def rms_norm(values, gain, epsilon):
    return values * lax.rsqrt(jnp.mean(values * values, axis=-1, keepdims=True) + epsilon) * gain


def unit_rows(field):
    return field * lax.rsqrt(jnp.sum(field * field, axis=-1, keepdims=True) + 1e-06)


def conv_masks(token_segments, taps):
    masks = []
    for shift in range(1, taps):
        earlier = jnp.concatenate([jnp.full((shift,), -1, jnp.int32), token_segments[:-shift]])
        masks.append((earlier == token_segments).astype(f32)[:, None])
    return masks


def short_conv(values, taps, masks):
    result = values * taps[0]
    for shift in range(1, taps.shape[0]):
        moved = jnp.concatenate([jnp.zeros((shift, values.shape[1]), f32), values[:-shift]], axis=0)
        result = result + moved * taps[shift] * masks[shift - 1]
    return result


def block_step(running_state, inputs):
    query_rows, key, value, beta, keep = inputs
    running_state = running_state * keep
    length = key.shape[1]
    strict = jnp.tril(jnp.ones((length, length), f32), -1)
    inclusive = jnp.tril(jnp.ones((length, length), f32))
    keyed = (
        jnp.einsum("hck,hdk->hcd", key * beta[:, :, None], key, precision=highest_precision)
        * strict
    )
    power = -keyed
    inverse = jnp.eye(length, dtype=f32) + power
    for level in range(length.bit_length() - 2):
        power = jnp.einsum("hcd,hde->hce", power, power, precision=highest_precision)
        inverse = inverse + jnp.einsum("hcd,hde->hce", inverse, power, precision=highest_precision)
    weights = inverse * beta[:, None, :]
    weighted_key = jnp.einsum("hcd,hdk->hck", weights, key, precision=highest_precision)
    weighted_value = jnp.einsum("kzw,kwp->kzp", weights, value, precision=highest_precision)
    fresh_values = weighted_value - jnp.einsum(
        "imd,ide->ime", weighted_key, running_state, precision=highest_precision
    )
    score_matrix = (
        jnp.einsum("hck,hdk->hcd", query_rows, key, precision=highest_precision) * inclusive
    )
    output_rows = jnp.einsum(
        "imd,ide->ime", query_rows, running_state, precision=highest_precision
    ) + jnp.einsum("kzw,kwp->kzp", score_matrix, fresh_values, precision=highest_precision)
    running_state = running_state + jnp.einsum(
        "sbi,sbw->siw", key, fresh_values, precision=highest_precision
    )
    return (running_state, output_rows)


def local_mixer(projected, beta_logit, conv_taps, gain, token_segments, keep):
    masks = conv_masks(token_segments, conv_taps.shape[1])
    heads = beta_logit.shape[1]
    length = projected.shape[1]
    width = projected.shape[2] // heads
    blocks = keep.shape[0]
    size = length // blocks
    parts = []
    for which in range(3):
        convolved = jax.nn.silu(short_conv(projected[which], conv_taps[which], masks))
        parts.append(convolved.reshape(length, heads, width))
    query_rows = unit_rows(parts[0]) * width ** (-0.5)
    key = unit_rows(parts[1])
    value = parts[2]
    beta = jax.nn.sigmoid(beta_logit)

    def arrange(field):
        return field.reshape(blocks, size, heads, width).transpose(0, 2, 1, 3)

    beta_blocks = beta.reshape(blocks, size, heads).transpose(0, 2, 1)
    initial = jnp.zeros((heads, width, width), f32)
    final, outputs = lax.scan(
        jax.checkpoint(block_step),
        initial,
        (arrange(query_rows), arrange(key), arrange(value), beta_blocks, keep),
    )
    outputs = outputs.transpose(0, 2, 1, 3).reshape(length, heads, width)
    return rms_norm(outputs, gain, 1e-05).reshape(length, heads * width)


def norm_rows(values, gain):
    return rms_norm(values, gain, 1e-06)


def dot(equation, left, right):
    return jnp.einsum(equation, left, right, preferred_element_type=f32)


def per_device(heads_axis, hidden_in, norm1_gain, qkv_weight, beta_weight, conv_weight, out_gain,
               out_weight, norm2_gain, gate_up_weight, down_weight, block_segments, cotangent):
    segments = block_segments[0]
    blocks = segments.shape[0]
    rows, model = hidden_in.shape
    shards = heads_axis
    length = rows * shards
    me = lax.axis_index("head")
    mine_z = lax.axis_index("z")

    def exchange(parts):
        return [parts[0]] + [
            lax.ppermute(parts[k], "head", [(i, i ^ k) for i in range(shards)])
            for k in range(1, shards)
        ]

    def gather_rows(own):
        return exchange([own] * shards)

    def scatter_sum(product):
        pieces = exchange([product[k * rows:(k + 1) * rows] for k in range(shards)])
        total = pieces[0].astype(f32)
        for piece in pieces[1:]:
            total = total + piece.astype(f32)
        return total

    def reorder(field, axis):
        pieces = [
            lax.dynamic_slice_in_dim(field, (me ^ k) * rows, rows, axis) for k in range(shards)
        ]
        return jnp.concatenate(pieces, axis)

    token_segments = jnp.repeat(segments, length // blocks)
    keep = jnp.concatenate(
        [jnp.zeros((1,), f32), (segments[1:] == segments[:-1]).astype(f32)]
    )
    hidden_parts = gather_rows(hidden_in)
    normed_all = jnp.concatenate(
        [norm_rows(part.astype(f32), norm1_gain).astype(bf16) for part in hidden_parts]
    )
    rows_in = hidden_in.astype(f32)
    cot_line = lax.all_gather(cotangent, "z", axis=0, tiled=True)
    hidden_line = lax.all_gather(hidden_in, "z", axis=0, tiled=True)
    line = cot_line.shape[0] // rows
    cot_every = jnp.concatenate(gather_rows(cot_line))
    hidden_every = jnp.stack(gather_rows(hidden_line)).reshape(shards, line, rows, model)

    projected = dot("td,sde->ste", normed_all, qkv_weight)
    beta_logit = dot("td,dh->th", normed_all, beta_weight)

    def mixer(projected_in, beta_in, conv_in, gain_in):
        return local_mixer(projected_in, beta_in, conv_in, gain_in, token_segments, keep)

    mixer_out, mixer_pull = jax.vjp(
        mixer, reorder(projected, 1), reorder(beta_logit, 0), conv_weight.astype(f32), out_gain
    )
    mixer_low = reorder(mixer_out.astype(bf16), 0)
    attn_rows = scatter_sum(dot("tc,cd->td", mixer_low, out_weight).astype(bf16))
    middle = rows_in + attn_rows
    normed_two, second_pull = jax.vjp(norm_rows, middle, norm2_gain)
    second_low = normed_two.astype(bf16)
    second_all = jnp.concatenate(gather_rows(second_low))
    second_line = lax.all_gather(second_low, "z", axis=0, tiled=True)
    second_every = jnp.concatenate(gather_rows(second_line))
    cot_all = lax.dynamic_index_in_dim(
        cot_every.reshape(shards, line, rows, model), mine_z, 1, False
    ).reshape(length, model)

    def feed_forward(second, cot):
        gate_up = dot("td,sdf->stf", second, gate_up_weight)
        sigmoid_gate = jax.nn.sigmoid(gate_up[0])
        silu_gate = gate_up[0] * sigmoid_gate
        hidden_low = (silu_gate * gate_up[1]).astype(bf16)
        hidden_grad = dot("td,fd->tf", cot, down_weight)
        gate_grad = hidden_grad * gate_up[1] * sigmoid_gate * (1.0 + gate_up[0] * (1.0 - sigmoid_gate))
        up_grad = hidden_grad * silu_gate
        return hidden_low, jnp.stack([gate_grad, up_grad]).astype(bf16)

    hidden_low, gate_up_low = feed_forward(second_all, cot_all)
    second_grad = scatter_sum(dot("stf,sdf->td", gate_up_low, gate_up_weight).astype(bf16))
    ffn_rows = scatter_sum(dot("tf,fd->td", hidden_low, down_weight).astype(bf16))
    block_out = (middle + ffn_rows).astype(bf16)
    middle_part, norm2_gain_grad = second_pull(second_grad)
    middle_grad = cotangent.astype(f32) + middle_part
    attn_grad_all = jnp.concatenate(gather_rows(middle_grad.astype(bf16)))
    mixer_in_grad = dot("td,cd->tc", attn_grad_all, out_weight)
    out_grad = dot("tc,td->cd", mixer_low, attn_grad_all).astype(bf16)

    hidden_every_low, gate_up_every = feed_forward(second_every, cot_every)
    down_grad = dot("tf,td->fd", hidden_every_low, cot_every).astype(bf16)
    gate_up_grad = dot("td,stf->sdf", second_every, gate_up_every).astype(bf16)

    projected_grad, beta_logit_grad, conv_grad, out_gain_grad = mixer_pull(reorder(mixer_in_grad, 0))
    projected_low = reorder(projected_grad.astype(bf16), 1)
    beta_low = reorder(beta_logit_grad.astype(bf16), 0)
    first_grad = scatter_sum(
        (dot("ste,sde->td", projected_low, qkv_weight) + dot("th,dh->td", beta_low, beta_weight)).astype(bf16)
    )
    r1 = lax.rsqrt(jnp.mean(rows_in * rows_in, axis=-1, keepdims=True) + 1e-06)
    m1 = rows_in * r1
    e1 = first_grad * norm1_gain
    norm1_gain_grad = jnp.sum(first_grad * m1, axis=0)
    input_grad = middle_grad + r1 * (e1 - m1 * jnp.mean(e1 * m1, axis=-1, keepdims=True))

    projected_line = lax.all_gather(projected_low, "z", axis=0)
    normed_every = norm_rows(hidden_every.astype(f32), norm1_gain).astype(bf16)
    normed_every = normed_every.transpose(1, 0, 2, 3).reshape(line, length, model)
    qkv_grad = dot("ztd,zste->sde", normed_every, projected_line).astype(bf16)
    beta_grad = dot("td,th->dh", normed_all, beta_low)

    def pair_sum(partial):
        other = lax.ppermute(partial, "core", [(0, 1), (1, 0)])
        return partial.astype(f32) + other.astype(f32)

    down_grad, gate_up_grad, qkv_grad = pair_sum(down_grad), pair_sum(gate_up_grad), pair_sum(qkv_grad)
    out_grad = lax.psum(out_grad, ("z", "core")).astype(f32)
    gains = jnp.concatenate([norm1_gain_grad, norm2_gain_grad, out_gain_grad])[None]
    gains = jnp.sum(lax.all_gather(gains, ("z", "core", "head"), axis=0, tiled=True), axis=0)
    small = jnp.concatenate([beta_grad.T.reshape(-1), conv_grad.reshape(-1)])[None]
    small = jnp.sum(lax.all_gather(small, ("z", "core"), axis=0, tiled=True), axis=0)
    beta_size = beta_grad.size
    beta_grad = small[:beta_size].reshape(beta_grad.shape[::-1]).T
    conv_grad = small[beta_size:].reshape(conv_grad.shape)
    return (
        block_out,
        input_grad,
        gains[:model],
        qkv_grad,
        beta_grad,
        conv_grad,
        gains[2 * model:],
        out_grad,
        gains[model:2 * model],
        gate_up_grad,
        down_grad,
    )


def solution(mesh):
    groups, shards = mesh.devices.shape
    split = Mesh(mesh.devices.reshape(groups // 2, 2, shards), ("z", "core", "head"))
    tokens = P(("z", "core", "head"), None)
    placed = (
        tokens,
        P(),
        P(None, None, "head"),
        P(None, "head"),
        P(None, None, "head"),
        P(),
        P("head", None),
        P(),
        P(None, None, "head"),
        P("head", None),
        P(("z", "core"), None),
        tokens,
    )
    return jax.shard_map(
        lambda *args: per_device(shards, *args),
        mesh=split,
        in_specs=placed,
        out_specs=(
            tokens,
            tokens,
            P(),
            P(None, None, "head"),
            P(None, "head"),
            P(None, None, "head"),
            P(),
            P("head", None),
            P(),
            P(None, None, "head"),
            P("head", None),
        ),
        check_vma=False,
    )
```

```python
import functools
import jax
import jax.numpy as jnp
from jax import lax
from jax.experimental import pallas as pl
from jax.experimental.pallas import tpu as pltpu
from jax.sharding import Mesh, PartitionSpec as P

f32 = jnp.float32
bf16 = jnp.bfloat16

DIMS = {"nn": (((1,), (0,)), ((), ())), "nt": (((1,), (1,)), ((), ())), "tn": (((0,), (0,)), ((), ()))}


def mm(left, right, form="nn"):
    return lax.dot_general(left.astype(bf16), right.astype(bf16), DIMS[form], preferred_element_type=f32)


def halves(value):
    high = value.astype(bf16)
    return high, (value - high.astype(f32)).astype(bf16)


def mm3(left, right, form="nn"):
    lh, ll = halves(left)
    rh, rl = halves(right)
    return mm(lh, rh, form) + (mm(lh, rl, form) + mm(ll, rh, form))


def sigmoid(value):
    return 1.0 / (1.0 + jnp.exp(-value))


def block_masks(length, size):
    row = lax.broadcasted_iota(jnp.int32, (length, length), 0)
    col = lax.broadcasted_iota(jnp.int32, (length, length), 1)
    same = (row ^ col) < size
    return (same & (row > col)), (same & (row >= col))


def keep_rows(info_ref, length, size):
    row = lax.broadcasted_iota(jnp.int32, (length, 1), 0)
    keep = jnp.zeros((length, 1), f32)
    for b in range(length // size):
        keep = jnp.where((row >= b * size) & (row < (b + 1) * size), info_ref[1 + b].astype(f32), keep)
    within = row & (size - 1)
    return [None] + [jnp.where(within >= shift, 1.0, keep) for shift in range(1, 4)]


def taken(ref, lead, me, rows, shards, cols):
    parts = []
    for j in range(shards):
        at = pl.ds(pl.multiple_of((me ^ j) * rows, rows), rows)
        parts.append(ref[lead + (at, cols)] if lead is not None else ref[at, cols])
    return jnp.concatenate(parts, 0)


def put(ref, lead, me, rows, shards, cols, value):
    for j in range(shards):
        at = pl.ds(pl.multiple_of((me ^ j) * rows, rows), rows)
        ref[lead + (at, cols)] = value[j * rows:(j + 1) * rows].astype(ref.dtype)


def forward_kernel(rows, shards, blocks, info_ref, proj_ref, logit_ref, taps_ref, gain_ref,
                   mixed_ref, conv_ref, o_ref, fresh_ref, state_ref, inv_ref,
                   q_s, k_s, u_s, w_s):
    length = rows * shards
    size = length // blocks
    heads = logit_ref.shape[1]
    width = proj_ref.shape[2] // heads
    me = info_ref[0]
    masks = keep_rows(info_ref, length, size)
    strict, inclusive = block_masks(length, size)
    logit = taken(logit_ref, (), me, rows, shards, slice(None))
    beta_all = sigmoid(logit)
    for h in range(heads):
        cols = slice(h * width, (h + 1) * width)
        beta = beta_all[:, h:h + 1]
        acts = []
        for s in range(3):
            x = taken(proj_ref, (s,), me, rows, shards, cols)
            z = x * taps_ref[4 * s:4 * s + 1, cols]
            for j in range(1, 4):
                z = z + pltpu.roll(x, j, 0) * (taps_ref[4 * s + j:4 * s + j + 1, cols] * masks[j])
            conv_ref[s, :, cols] = z
            acts.append(z * sigmoid(z))
        q0, k0, v = acts
        q = q0 * (lax.rsqrt(jnp.sum(q0 * q0, axis=-1, keepdims=True) + 1e-06) * width ** -0.5)
        k = k0 * lax.rsqrt(jnp.sum(k0 * k0, axis=-1, keepdims=True) + 1e-06)
        q_s[:, cols] = q
        k_s[:, cols] = k
        power = jnp.where(strict, mm3(k * -beta, k, "nt"), 0.0)
        inverse = power
        step = 1
        while 2 * step < size:
            power = mm3(power, power)
            inverse = inverse + power + mm3(inverse, power)
            step *= 2
        inv_ref[h] = inverse
        bk, bv = beta * k, beta * v
        w_s[:, cols] = bk + mm(inverse, bk)
        u_s[:, cols] = bv + mm(inverse, bv)
    states = [jnp.zeros((width, width), f32)] * heads
    for b in range(blocks):
        at = slice(b * size, (b + 1) * size)
        keep = info_ref[1 + b].astype(f32)
        for h in range(heads):
            cols = slice(h * width, (h + 1) * width)
            state = states[h] * keep
            state_ref[h, b] = state
            fresh = u_s[at, cols] - mm(w_s[at, cols], state)
            fresh_ref[at, cols] = fresh
            states[h] = state + mm(k_s[at, cols], fresh, "tn")
            o_ref[at, cols] = mm(q_s[at, cols], state)
    for h in range(heads):
        cols = slice(h * width, (h + 1) * width)
        scores = jnp.where(inclusive, mm(q_s[:, cols], k_s[:, cols], "nt"), 0.0)
        o = o_ref[:, cols] + mm(scores, fresh_ref[:, cols])
        o_ref[:, cols] = o
        mixed = o * lax.rsqrt(jnp.mean(o * o, axis=-1, keepdims=True) + 1e-05) * gain_ref[0:1, :]
        put(mixed_ref, (), me, rows, shards, cols, mixed)


def backward_kernel(rows, shards, blocks, info_ref, grad_ref, proj_ref, logit_ref, taps_ref, gain_ref,
                    conv_ref, o_ref, fresh_ref, state_ref, inv_ref,
                    proj_grad_ref, logit_grad_ref, taps_grad_ref, gain_grad_ref,
                    q_s, k_s, w_s, do_s, df_s, dq_s, dk_s):
    length = rows * shards
    size = length // blocks
    heads = logit_ref.shape[1]
    width = proj_ref.shape[2] // heads
    me = info_ref[0]
    masks = keep_rows(info_ref, length, size)
    strict, inclusive = block_masks(length, size)
    logit = taken(logit_ref, (), me, rows, shards, slice(None))
    beta_all = sigmoid(logit)
    gain_total = jnp.zeros((1, width), f32)
    lane = lax.broadcasted_iota(jnp.int32, (length, logit_grad_ref.shape[1]), 1)
    logit_grad = jnp.zeros((length, logit_grad_ref.shape[1]), f32)
    for h in range(heads):
        cols = slice(h * width, (h + 1) * width)
        beta = beta_all[:, h:h + 1]
        zq, zk = conv_ref[0, :, cols], conv_ref[1, :, cols]
        q0, k0 = zq * sigmoid(zq), zk * sigmoid(zk)
        q = q0 * (lax.rsqrt(jnp.sum(q0 * q0, axis=-1, keepdims=True) + 1e-06) * width ** -0.5)
        k = k0 * lax.rsqrt(jnp.sum(k0 * k0, axis=-1, keepdims=True) + 1e-06)
        q_s[:, cols] = q
        k_s[:, cols] = k
        bk = beta * k
        w_s[:, cols] = bk + mm(inv_ref[h], bk)
        g = taken(grad_ref, (), me, rows, shards, cols)
        o = o_ref[:, cols]
        r = lax.rsqrt(jnp.mean(o * o, axis=-1, keepdims=True) + 1e-05)
        on = o * r
        gain_total = gain_total + jnp.sum(g * on, axis=0, keepdims=True)
        dn = g * gain_ref[0:1, :]
        do = r * (dn - on * jnp.mean(dn * on, axis=-1, keepdims=True))
        do_s[:, cols] = do
        scores = jnp.where(inclusive, mm(q, k, "nt"), 0.0)
        df_s[:, cols] = mm(scores, do, "tn")
        dscores = jnp.where(inclusive, mm(do, fresh_ref[:, cols], "nt"), 0.0)
        dq_s[:, cols] = mm(dscores, k)
        dk_s[:, cols] = mm(dscores, q, "tn")
    gain_grad_ref[...] = jnp.broadcast_to(gain_total, gain_grad_ref.shape)
    carried = [jnp.zeros((width, width), f32)] * heads
    for b in reversed(range(blocks)):
        at = slice(b * size, (b + 1) * size)
        keep = info_ref[1 + b].astype(f32)
        for h in range(heads):
            cols = slice(h * width, (h + 1) * width)
            after = carried[h]
            df = df_s[at, cols] + mm(k_s[at, cols], after)
            df_s[at, cols] = df
            do = do_s[at, cols]
            carried[h] = keep * (after + mm(q_s[at, cols], do, "tn") - mm(w_s[at, cols], df, "tn"))
            dq_s[at, cols] = dq_s[at, cols] + mm(do, state_ref[h, b], "nt")
            dk_s[at, cols] = dk_s[at, cols] + mm(fresh_ref[at, cols], after, "nt")
    for h in range(heads):
        cols = slice(h * width, (h + 1) * width)
        beta = beta_all[:, h:h + 1]
        k = k_s[:, cols]
        df = df_s[:, cols]
        dr = df + mm(inv_ref[h], df, "tn")
        bdr = beta * dr
        fresh = fresh_ref[:, cols]
        lower = jnp.where(strict, mm(dr, fresh, "nt"), 0.0)
        blower = beta * lower
        zv = conv_ref[2, :, cols]
        sv = sigmoid(zv)
        held, back = [], []
        for b in range(blocks):
            at = slice(b * size, (b + 1) * size)
            held.append(mm(k[at], state_ref[h, b]))
            back.append(mm(bdr[at], state_ref[h, b], "nt"))
        excess = zv * sv - jnp.concatenate(held, 0)
        gram = mm(k, k, "nt")
        dbeta = jnp.sum(dr * excess, axis=-1, keepdims=True) - jnp.sum(lower * gram, axis=-1, keepdims=True)
        logit_grad = jnp.where(lane == h, dbeta * beta * (1.0 - beta), logit_grad)
        dk = dk_s[:, cols] - jnp.concatenate(back, 0) - (mm(blower, k) + mm(blower, k, "tn"))
        dq = dq_s[:, cols]
        for s, dy in ((0, dq), (1, dk), (2, bdr)):
            z = conv_ref[s, :, cols]
            sz = sigmoid(z)
            if s < 2:
                y = z * sz
                r = lax.rsqrt(jnp.sum(y * y, axis=-1, keepdims=True) + 1e-06)
                yn = y * r
                if s == 0:
                    r = r * width ** -0.5
                dy = r * (dy - yn * jnp.sum(dy * yn, axis=-1, keepdims=True))
            dz = dy * sz * (1.0 + z * (1.0 - sz))
            x = taken(proj_ref, (s,), me, rows, shards, cols)
            dx = dz * taps_ref[4 * s:4 * s + 1, cols]
            taps_grad_ref[4 * s:4 * s + 1, cols] = jnp.sum(dz * x, axis=0, keepdims=True)
            for j in range(1, 4):
                moved = dz * masks[j]
                taps_grad_ref[4 * s + j:4 * s + j + 1, cols] = jnp.sum(moved * pltpu.roll(x, j, 0), axis=0, keepdims=True)
                dx = dx + pltpu.roll(moved, length - j, 0) * taps_ref[4 * s + j:4 * s + j + 1, cols]
            put(proj_grad_ref, (s,), me, rows, shards, cols, dx)
    put(logit_grad_ref, (), me, rows, shards, slice(None), logit_grad)


SMEM = pl.BlockSpec(memory_space=pltpu.SMEM)
VMEM = pl.BlockSpec(memory_space=pltpu.VMEM)


def mixer_forward(info, projected, logit, taps, gain, rows, shards, blocks):
    _, length, span = projected.shape
    heads = logit.shape[1]
    width = span // heads
    shape = jax.ShapeDtypeStruct
    return pl.pallas_call(
        functools.partial(forward_kernel, rows, shards, blocks),
        out_shape=(
            shape((length, span), bf16),
            shape((3, length, span), f32),
            shape((length, span), f32),
            shape((length, span), f32),
            shape((heads, blocks, width, width), f32),
            shape((heads, length, length), f32),
        ),
        in_specs=[SMEM] + [VMEM] * 4,
        out_specs=(VMEM,) * 6,
        scratch_shapes=[pltpu.VMEM((length, span), f32)] * 4,
        compiler_params=pltpu.CompilerParams(vmem_limit_bytes=48 * 1024 * 1024),
        cost_estimate=pl.CostEstimate(flops=10**10, bytes_accessed=10 * 2**20, transcendentals=10**6),
        name="mixer_forward",
    )(info, projected, logit, taps, gain)


def mixer_backward(info, grad, projected, logit, taps, gain, saved, rows, shards, blocks):
    _, length, span = projected.shape
    heads = logit.shape[1]
    width = span // heads
    shape = jax.ShapeDtypeStruct
    return pl.pallas_call(
        functools.partial(backward_kernel, rows, shards, blocks),
        out_shape=(
            shape((3, length, span), bf16),
            shape((length, 128), f32),
            shape((16, span), f32),
            shape((8, width), f32),
        ),
        in_specs=[SMEM] + [VMEM] * 10,
        out_specs=(VMEM,) * 4,
        scratch_shapes=[pltpu.VMEM((length, span), f32)] * 7,
        compiler_params=pltpu.CompilerParams(vmem_limit_bytes=48 * 1024 * 1024),
        cost_estimate=pl.CostEstimate(flops=2 * 10**10, bytes_accessed=14 * 2**20, transcendentals=10**6),
        name="mixer_backward",
    )(info, grad, projected, logit, taps, gain, *saved)


def norm_rows(values, gain):
    return values * lax.rsqrt(jnp.mean(values * values, axis=-1, keepdims=True) + 1e-06) * gain


def norm_back(grad, values, gain):
    scale = lax.rsqrt(jnp.mean(values * values, axis=-1, keepdims=True) + 1e-06)
    unit = values * scale
    inner = grad * gain
    back = scale * (inner - unit * jnp.mean(inner * unit, axis=-1, keepdims=True))
    return back, jnp.sum(grad * unit, axis=0)


def dot(equation, left, right):
    return jnp.einsum(equation, left, right, preferred_element_type=f32)


def after(value, *others):
    return lax.optimization_barrier((value, *others))[0]


def per_device(shards, hidden_in, norm1_gain, qkv_weight, beta_weight, conv_weight, out_gain,
               out_weight, norm2_gain, gate_up_weight, down_weight, block_segments, cotangent):
    segments = block_segments[0]
    blocks = segments.shape[0]
    rows, model = hidden_in.shape
    length = rows * shards
    me = lax.axis_index("head")
    mine_z = lax.axis_index("z")

    def exchange(parts):
        return [parts[0]] + [
            lax.ppermute(parts[k], "head", [(i, i ^ k) for i in range(shards)])
            for k in range(1, shards)
        ]

    def gather_rows(own):
        return exchange([own] * shards)

    def scatter_sum(product):
        pieces = exchange([product[k * rows:(k + 1) * rows] for k in range(shards)])
        total = pieces[0].astype(f32)
        for piece in pieces[1:]:
            total = total + piece.astype(f32)
        return total

    keep = jnp.concatenate([jnp.zeros((1,), bool), segments[1:] == segments[:-1]])
    info = jnp.concatenate([me[None], keep]).astype(jnp.int32)
    taps = conv_weight.astype(f32).reshape(-1, conv_weight.shape[2])
    taps = jnp.pad(taps, ((0, 16 - taps.shape[0]), (0, 0)))
    gain = out_gain[None]

    hidden_parts = gather_rows(hidden_in)
    normed_all = jnp.concatenate(
        [norm_rows(part.astype(f32), norm1_gain).astype(bf16) for part in hidden_parts]
    )
    rows_in = hidden_in.astype(f32)
    cot_all = jnp.concatenate(gather_rows(cotangent))
    cot_line = lax.all_gather(cotangent, "z", axis=0, tiled=True)
    hidden_line = lax.all_gather(hidden_in, "z", axis=0, tiled=True)
    line = cot_line.shape[0] // rows

    projected = dot("td,sde->ste", normed_all, qkv_weight)
    beta_logit = dot("td,dh->th", normed_all, beta_weight)
    mixer_low, *saved = mixer_forward(info, projected, beta_logit, taps, gain, rows, shards, blocks)
    attn_rows = scatter_sum(dot("tc,cd->td", mixer_low, out_weight).astype(bf16))
    middle = rows_in + attn_rows
    second_low = norm_rows(middle, norm2_gain).astype(bf16)
    second_all = jnp.concatenate(gather_rows(second_low))
    second_line = lax.all_gather(second_low, "z", axis=0, tiled=True)

    def feed_forward(second, cot):
        gate_up = dot("td,sdf->stf", second, gate_up_weight)
        sigmoid_gate = jax.nn.sigmoid(gate_up[0])
        silu_gate = gate_up[0] * sigmoid_gate
        hidden_low = (silu_gate * gate_up[1]).astype(bf16)
        hidden_grad = dot("td,fd->tf", cot, down_weight)
        gate_grad = hidden_grad * gate_up[1] * sigmoid_gate * (1.0 + gate_up[0] * (1.0 - sigmoid_gate))
        up_grad = hidden_grad * silu_gate
        return hidden_low, jnp.stack([gate_grad, up_grad]).astype(bf16)

    hidden_low, gate_up_low = feed_forward(second_all, cot_all)
    second_grad = scatter_sum(dot("stf,sdf->td", gate_up_low, gate_up_weight).astype(bf16))
    ffn_rows = scatter_sum(dot("tf,fd->td", hidden_low, down_weight).astype(bf16))
    block_out = (middle + ffn_rows).astype(bf16)
    middle_part, norm2_gain_grad = norm_back(second_grad, middle, norm2_gain)
    middle_grad = cotangent.astype(f32) + middle_part
    attn_grad_all = jnp.concatenate(gather_rows(middle_grad.astype(bf16)))
    mixer_in_grad = dot("td,cd->tc", attn_grad_all, out_weight)
    out_grad = dot("tc,td->cd", mixer_low, attn_grad_all).astype(bf16)
    mixer_in_grad = after(mixer_in_grad, out_grad)

    projected_low, beta_logit_grad, conv_grad, out_gain_grad = mixer_backward(
        info, mixer_in_grad, projected, beta_logit, taps, gain, saved, rows, shards, blocks
    )
    beta_low = beta_logit_grad[:, :beta_weight.shape[1]].astype(bf16)
    first_grad = scatter_sum(
        (dot("ste,sde->td", projected_low, qkv_weight) + dot("th,dh->td", beta_low, beta_weight)).astype(bf16)
    )
    rows_part, norm1_gain_grad = norm_back(first_grad, rows_in, norm1_gain)
    input_grad = middle_grad + rows_part
    projected_line = lax.all_gather(projected_low, "z", axis=0)
    beta_grad = dot("td,th->dh", normed_all, beta_low)

    cot_every = jnp.concatenate(gather_rows(cot_line))
    second_every = jnp.concatenate(gather_rows(second_line))
    hidden_every_low, gate_up_every = feed_forward(second_every, cot_every)

    def pair_sum(partial):
        other = lax.ppermute(partial, "core", [(0, 1), (1, 0)])
        return partial.astype(f32) + other.astype(f32)

    gate_up_grad = jnp.stack(
        [pair_sum(dot("td,tf->df", second_every, gate_up_every[s]).astype(bf16)) for s in range(2)]
    )
    down_grad = pair_sum(dot("tf,td->fd", hidden_every_low, cot_every).astype(bf16))
    hidden_every = jnp.stack(gather_rows(hidden_line)).reshape(shards, line, rows, model)
    normed_every = norm_rows(hidden_every.astype(f32), norm1_gain).astype(bf16)
    normed_every = normed_every.transpose(1, 0, 2, 3).reshape(line, length, model)
    qkv_grad = jnp.stack(
        [pair_sum(dot("ztd,zte->de", normed_every, projected_line[:, s]).astype(bf16)) for s in range(3)]
    )
    out_grad = lax.psum(out_grad, ("z", "core")).astype(f32)

    gains = jnp.concatenate([norm1_gain_grad, norm2_gain_grad, out_gain_grad[0]])
    small = jnp.concatenate([gains, beta_grad.T.reshape(-1), conv_grad[:12].reshape(-1)])
    small = small.reshape(-1, 128)

    def butterfly(value, axis, size):
        step = 1
        while step < size:
            value = value + lax.ppermute(value, axis, [(i, i ^ step) for i in range(size)])
            step *= 2
        return value

    small = butterfly(butterfly(small, "core", 2), "z", line).reshape(-1)
    gain_size = gains.size
    gains = butterfly(small[:gain_size].reshape(-1, 128), "head", shards).reshape(-1)
    beta_size = beta_grad.size
    beta_grad = small[gain_size:gain_size + beta_size].reshape(beta_grad.shape[::-1]).T
    conv_grad = small[gain_size + beta_size:].reshape(conv_weight.shape)
    return (
        block_out,
        input_grad,
        gains[:model],
        qkv_grad,
        beta_grad,
        conv_grad,
        gains[2 * model:],
        out_grad,
        gains[model:2 * model],
        gate_up_grad,
        down_grad,
    )


def solution(mesh):
    groups, shards = mesh.devices.shape
    split = Mesh(mesh.devices.reshape(groups // 2, 2, shards), ("z", "core", "head"))
    tokens = P(("z", "core", "head"), None)
    placed = (
        tokens,
        P(),
        P(None, None, "head"),
        P(None, "head"),
        P(None, None, "head"),
        P(),
        P("head", None),
        P(),
        P(None, None, "head"),
        P("head", None),
        P(("z", "core"), None),
        tokens,
    )
    return jax.shard_map(
        lambda *args: per_device(shards, *args),
        mesh=split,
        in_specs=placed,
        out_specs=(
            tokens,
            tokens,
            P(),
            P(None, None, "head"),
            P(None, "head"),
            P(None, None, "head"),
            P(),
            P("head", None),
            P(),
            P(None, None, "head"),
            P("head", None),
        ),
        check_vma=False,
    )
```

```python
import functools
import jax
import jax.numpy as jnp
from jax import lax
from jax.experimental import pallas as pl
from jax.experimental.pallas import tpu as pltpu
from jax.sharding import Mesh, PartitionSpec as P

f32 = jnp.float32
bf16 = jnp.bfloat16

DIMS = {"nn": (((1,), (0,)), ((), ())), "nt": (((1,), (1,)), ((), ())), "tn": (((0,), (0,)), ((), ()))}


def mm(left, right, form="nn"):
    return lax.dot_general(left.astype(bf16), right.astype(bf16), DIMS[form], preferred_element_type=f32)


def halves(value):
    high = value.astype(bf16)
    return high, (value - high.astype(f32)).astype(bf16)


def mm3(left, right, form="nn"):
    lh, ll = halves(left)
    rh, rl = halves(right)
    return mm(lh, rh, form) + (mm(lh, rl, form) + mm(ll, rh, form))


def sigmoid(value):
    return 1.0 / (1.0 + jnp.exp(-value))


def block_masks(length, size):
    row = lax.broadcasted_iota(jnp.int32, (length, length), 0)
    col = lax.broadcasted_iota(jnp.int32, (length, length), 1)
    same = (row ^ col) < size
    return (same & (row > col)), (same & (row >= col))


def keep_rows(info_ref, length, size):
    row = lax.broadcasted_iota(jnp.int32, (length, 1), 0)
    keep = jnp.zeros((length, 1), f32)
    for b in range(length // size):
        keep = jnp.where((row >= b * size) & (row < (b + 1) * size), info_ref[1 + b].astype(f32), keep)
    within = row & (size - 1)
    return [None] + [jnp.where(within >= shift, 1.0, keep) for shift in range(1, 4)]


def taken(ref, lead, me, rows, shards, cols):
    parts = []
    for j in range(shards):
        at = pl.ds(pl.multiple_of((me ^ j) * rows, rows), rows)
        parts.append(ref[lead + (at, cols)] if lead is not None else ref[at, cols])
    return jnp.concatenate(parts, 0)


def put(ref, lead, me, rows, shards, cols, value):
    for j in range(shards):
        at = pl.ds(pl.multiple_of((me ^ j) * rows, rows), rows)
        ref[lead + (at, cols)] = value[j * rows:(j + 1) * rows].astype(ref.dtype)


def forward_kernel(rows, shards, blocks, info_ref, proj_ref, logit_ref, taps_ref, gain_ref,
                   mixed_ref, conv_ref, o_ref, fresh_ref, state_ref, inv_ref,
                   q_s, k_s, u_s, w_s):
    length = rows * shards
    size = length // blocks
    heads = logit_ref.shape[1]
    width = proj_ref.shape[2] // heads
    me = info_ref[0]
    masks = keep_rows(info_ref, length, size)
    strict, inclusive = block_masks(length, size)
    logit = taken(logit_ref, (), me, rows, shards, slice(None))
    beta_all = sigmoid(logit)
    for h in range(heads):
        cols = slice(h * width, (h + 1) * width)
        beta = beta_all[:, h:h + 1]
        acts = []
        for s in range(3):
            x = taken(proj_ref, (s,), me, rows, shards, cols)
            z = x * taps_ref[4 * s:4 * s + 1, cols]
            for j in range(1, 4):
                z = z + pltpu.roll(x, j, 0) * (taps_ref[4 * s + j:4 * s + j + 1, cols] * masks[j])
            conv_ref[s, :, cols] = z
            acts.append(z * sigmoid(z))
        q0, k0, v = acts
        q = q0 * (lax.rsqrt(jnp.sum(q0 * q0, axis=-1, keepdims=True) + 1e-06) * width ** -0.5)
        k = k0 * lax.rsqrt(jnp.sum(k0 * k0, axis=-1, keepdims=True) + 1e-06)
        q_s[:, cols] = q
        k_s[:, cols] = k
        power = jnp.where(strict, mm3(k * -beta, k, "nt"), 0.0)
        inverse = power
        step = 1
        while 2 * step < size:
            power = mm3(power, power)
            inverse = inverse + power + mm3(inverse, power)
            step *= 2
        inv_ref[h] = inverse
        bk, bv = beta * k, beta * v
        w_s[:, cols] = bk + mm(inverse, bk)
        u_s[:, cols] = bv + mm(inverse, bv)
    states = [jnp.zeros((width, width), f32)] * heads
    for b in range(blocks):
        at = slice(b * size, (b + 1) * size)
        keep = info_ref[1 + b].astype(f32)
        for h in range(heads):
            cols = slice(h * width, (h + 1) * width)
            state = states[h] * keep
            state_ref[h, b] = state
            fresh = u_s[at, cols] - mm(w_s[at, cols], state)
            fresh_ref[at, cols] = fresh
            states[h] = state + mm(k_s[at, cols], fresh, "tn")
            o_ref[at, cols] = mm(q_s[at, cols], state)
    for h in range(heads):
        cols = slice(h * width, (h + 1) * width)
        scores = jnp.where(inclusive, mm(q_s[:, cols], k_s[:, cols], "nt"), 0.0)
        o = o_ref[:, cols] + mm(scores, fresh_ref[:, cols])
        o_ref[:, cols] = o
        mixed = o * lax.rsqrt(jnp.mean(o * o, axis=-1, keepdims=True) + 1e-05) * gain_ref[0:1, :]
        put(mixed_ref, (), me, rows, shards, cols, mixed)


def backward_kernel(rows, shards, blocks, info_ref, grad_ref, proj_ref, logit_ref, taps_ref, gain_ref,
                    conv_ref, o_ref, fresh_ref, state_ref, inv_ref,
                    proj_grad_ref, logit_grad_ref, taps_grad_ref, gain_grad_ref,
                    q_s, k_s, w_s, do_s, df_s, dq_s, dk_s):
    length = rows * shards
    size = length // blocks
    heads = logit_ref.shape[1]
    width = proj_ref.shape[2] // heads
    me = info_ref[0]
    masks = keep_rows(info_ref, length, size)
    strict, inclusive = block_masks(length, size)
    logit = taken(logit_ref, (), me, rows, shards, slice(None))
    beta_all = sigmoid(logit)
    gain_total = jnp.zeros((1, width), f32)
    lane = lax.broadcasted_iota(jnp.int32, (length, logit_grad_ref.shape[1]), 1)
    logit_grad = jnp.zeros((length, logit_grad_ref.shape[1]), f32)
    for h in range(heads):
        cols = slice(h * width, (h + 1) * width)
        beta = beta_all[:, h:h + 1]
        zq, zk = conv_ref[0, :, cols], conv_ref[1, :, cols]
        q0, k0 = zq * sigmoid(zq), zk * sigmoid(zk)
        q = q0 * (lax.rsqrt(jnp.sum(q0 * q0, axis=-1, keepdims=True) + 1e-06) * width ** -0.5)
        k = k0 * lax.rsqrt(jnp.sum(k0 * k0, axis=-1, keepdims=True) + 1e-06)
        q_s[:, cols] = q
        k_s[:, cols] = k
        bk = beta * k
        w_s[:, cols] = bk + mm(inv_ref[h], bk)
        g = taken(grad_ref, (), me, rows, shards, cols)
        o = o_ref[:, cols]
        r = lax.rsqrt(jnp.mean(o * o, axis=-1, keepdims=True) + 1e-05)
        on = o * r
        gain_total = gain_total + jnp.sum(g * on, axis=0, keepdims=True)
        dn = g * gain_ref[0:1, :]
        do = r * (dn - on * jnp.mean(dn * on, axis=-1, keepdims=True))
        do_s[:, cols] = do
        scores = jnp.where(inclusive, mm(q, k, "nt"), 0.0)
        df_s[:, cols] = mm(scores, do, "tn")
        dscores = jnp.where(inclusive, mm(do, fresh_ref[:, cols], "nt"), 0.0)
        dq_s[:, cols] = mm(dscores, k)
        dk_s[:, cols] = mm(dscores, q, "tn")
    gain_grad_ref[...] = jnp.broadcast_to(gain_total, gain_grad_ref.shape)
    carried = [jnp.zeros((width, width), f32)] * heads
    for b in reversed(range(blocks)):
        at = slice(b * size, (b + 1) * size)
        keep = info_ref[1 + b].astype(f32)
        for h in range(heads):
            cols = slice(h * width, (h + 1) * width)
            after = carried[h]
            df = df_s[at, cols] + mm(k_s[at, cols], after)
            df_s[at, cols] = df
            do = do_s[at, cols]
            carried[h] = keep * (after + mm(q_s[at, cols], do, "tn") - mm(w_s[at, cols], df, "tn"))
            dq_s[at, cols] = dq_s[at, cols] + mm(do, state_ref[h, b], "nt")
            dk_s[at, cols] = dk_s[at, cols] + mm(fresh_ref[at, cols], after, "nt")
    for h in range(heads):
        cols = slice(h * width, (h + 1) * width)
        beta = beta_all[:, h:h + 1]
        k = k_s[:, cols]
        df = df_s[:, cols]
        dr = df + mm(inv_ref[h], df, "tn")
        bdr = beta * dr
        fresh = fresh_ref[:, cols]
        lower = jnp.where(strict, mm(dr, fresh, "nt"), 0.0)
        blower = beta * lower
        zv = conv_ref[2, :, cols]
        sv = sigmoid(zv)
        held, back = [], []
        for b in range(blocks):
            at = slice(b * size, (b + 1) * size)
            held.append(mm(k[at], state_ref[h, b]))
            back.append(mm(bdr[at], state_ref[h, b], "nt"))
        excess = zv * sv - jnp.concatenate(held, 0)
        gram = mm(k, k, "nt")
        dbeta = jnp.sum(dr * excess, axis=-1, keepdims=True) - jnp.sum(lower * gram, axis=-1, keepdims=True)
        logit_grad = jnp.where(lane == h, dbeta * beta * (1.0 - beta), logit_grad)
        dk = dk_s[:, cols] - jnp.concatenate(back, 0) - (mm(blower, k) + mm(blower, k, "tn"))
        dq = dq_s[:, cols]
        for s, dy in ((0, dq), (1, dk), (2, bdr)):
            z = conv_ref[s, :, cols]
            sz = sigmoid(z)
            if s < 2:
                y = z * sz
                r = lax.rsqrt(jnp.sum(y * y, axis=-1, keepdims=True) + 1e-06)
                yn = y * r
                if s == 0:
                    r = r * width ** -0.5
                dy = r * (dy - yn * jnp.sum(dy * yn, axis=-1, keepdims=True))
            dz = dy * sz * (1.0 + z * (1.0 - sz))
            x = taken(proj_ref, (s,), me, rows, shards, cols)
            dx = dz * taps_ref[4 * s:4 * s + 1, cols]
            taps_grad_ref[4 * s:4 * s + 1, cols] = jnp.sum(dz * x, axis=0, keepdims=True)
            for j in range(1, 4):
                moved = dz * masks[j]
                taps_grad_ref[4 * s + j:4 * s + j + 1, cols] = jnp.sum(moved * pltpu.roll(x, j, 0), axis=0, keepdims=True)
                dx = dx + pltpu.roll(moved, length - j, 0) * taps_ref[4 * s + j:4 * s + j + 1, cols]
            put(proj_grad_ref, (s,), me, rows, shards, cols, dx)
    put(logit_grad_ref, (), me, rows, shards, slice(None), logit_grad)


SMEM = pl.BlockSpec(memory_space=pltpu.SMEM)
VMEM = pl.BlockSpec(memory_space=pltpu.VMEM)


def mixer_forward(info, projected, logit, taps, gain, rows, shards, blocks):
    _, length, span = projected.shape
    heads = logit.shape[1]
    width = span // heads
    shape = jax.ShapeDtypeStruct
    return pl.pallas_call(
        functools.partial(forward_kernel, rows, shards, blocks),
        out_shape=(
            shape((length, span), bf16),
            shape((3, length, span), f32),
            shape((length, span), f32),
            shape((length, span), f32),
            shape((heads, blocks, width, width), f32),
            shape((heads, length, length), f32),
        ),
        in_specs=[SMEM] + [VMEM] * 4,
        out_specs=(VMEM,) * 6,
        scratch_shapes=[pltpu.VMEM((length, span), f32)] * 4,
        compiler_params=pltpu.CompilerParams(vmem_limit_bytes=48 * 1024 * 1024),
        cost_estimate=pl.CostEstimate(flops=10**10, bytes_accessed=10 * 2**20, transcendentals=10**6),
        name="mixer_forward",
    )(info, projected, logit, taps, gain)


def mixer_backward(info, grad, projected, logit, taps, gain, saved, rows, shards, blocks):
    _, length, span = projected.shape
    heads = logit.shape[1]
    width = span // heads
    shape = jax.ShapeDtypeStruct
    return pl.pallas_call(
        functools.partial(backward_kernel, rows, shards, blocks),
        out_shape=(
            shape((3, length, span), bf16),
            shape((length, 128), f32),
            shape((16, span), f32),
            shape((8, width), f32),
        ),
        in_specs=[SMEM] + [VMEM] * 10,
        out_specs=(VMEM,) * 4,
        scratch_shapes=[pltpu.VMEM((length, span), f32)] * 7,
        compiler_params=pltpu.CompilerParams(vmem_limit_bytes=48 * 1024 * 1024),
        cost_estimate=pl.CostEstimate(flops=2 * 10**10, bytes_accessed=14 * 2**20, transcendentals=10**6),
        name="mixer_backward",
    )(info, grad, projected, logit, taps, gain, *saved)


def pair_kernel(planes, *refs):
    out_ref = refs[-1]
    for s in range(planes):
        total = refs[2 * s][...].astype(f32) + refs[2 * s + 1][...].astype(f32)
        if planes == 1:
            out_ref[...] = total
        else:
            out_ref[s] = total


def pair_sum(partials):
    others = [lax.ppermute(partial, "core", [(0, 1), (1, 0)]) for partial in partials]
    planes = len(partials)
    height, span = partials[0].shape
    tile = 256 if height % 256 == 0 else 128
    shape = (height, span) if planes == 1 else (planes, height, span)
    block = (tile, span) if planes == 1 else (planes, tile, span)
    return pl.pallas_call(
        functools.partial(pair_kernel, planes),
        grid=(height // tile,),
        out_shape=jax.ShapeDtypeStruct(shape, f32),
        in_specs=[pl.BlockSpec((tile, span), lambda i: (i, 0))] * (2 * planes),
        out_specs=pl.BlockSpec(block, (lambda i: (i, 0)) if planes == 1 else (lambda i: (0, i, 0))),
        compiler_params=pltpu.CompilerParams(vmem_limit_bytes=32 * 1024 * 1024),
        cost_estimate=pl.CostEstimate(
            flops=planes * height * span, bytes_accessed=8 * planes * height * span, transcendentals=0),
        name="pair_sum",
    )(*[ref for pair in zip(partials, others) for ref in pair])


def planes_kernel(pieces, *refs):
    out_ref = refs[2 * pieces]
    total = None
    for p in range(pieces):
        term = lax.dot_general(refs[p][...], refs[pieces + p][0], DIMS["tn"], preferred_element_type=f32)
        total = term if total is None else total + term
    out_ref[0] = total


def planes_grad(lefts, rights, tile=256):
    pieces = len(lefts)
    height = lefts[0].shape[1]
    planes, depth, span = rights[0].shape
    return pl.pallas_call(
        functools.partial(planes_kernel, pieces),
        grid=(planes, height // tile),
        out_shape=jax.ShapeDtypeStruct((planes, height, span), f32),
        in_specs=[pl.BlockSpec((depth, tile), lambda s, i: (0, i))] * pieces
        + [pl.BlockSpec((1, depth, span), lambda s, i: (s, 0, 0))] * pieces,
        out_specs=pl.BlockSpec((1, tile, span), lambda s, i: (s, i, 0)),
        compiler_params=pltpu.CompilerParams(vmem_limit_bytes=48 * 1024 * 1024),
        cost_estimate=pl.CostEstimate(
            flops=2 * pieces * depth * planes * height * span,
            bytes_accessed=4 * planes * height * span, transcendentals=0),
        name="planes_grad",
    )(*lefts, *rights)


def turned_kernel(pieces, *refs):
    out_ref = refs[2 * pieces]
    turned = refs[2 * pieces + 1:]

    @pl.when(pl.program_id(0) == 0)
    def _():
        for p in range(pieces):
            turned[p][...] = refs[p][...].T

    total = None
    for p in range(pieces):
        term = jnp.dot(turned[p][...], refs[pieces + p][...], preferred_element_type=f32)
        total = term if total is None else total + term
    out_ref[...] = total


def turned_grad(lefts, rights, tile=256):
    pieces = len(lefts)
    depth, height = lefts[0].shape
    span = rights[0].shape[1]
    return pl.pallas_call(
        functools.partial(turned_kernel, pieces),
        grid=(span // tile,),
        out_shape=jax.ShapeDtypeStruct((height, span), f32),
        in_specs=[pl.BlockSpec((depth, height), lambda i: (0, 0), pipeline_mode=pl.Buffered(1))] * pieces
        + [pl.BlockSpec((depth, tile), lambda i: (0, i))] * pieces,
        out_specs=pl.BlockSpec((height, tile), lambda i: (0, i)),
        scratch_shapes=[pltpu.VMEM((height, depth), bf16)] * pieces,
        compiler_params=pltpu.CompilerParams(vmem_limit_bytes=48 * 1024 * 1024),
        cost_estimate=pl.CostEstimate(
            flops=2 * pieces * depth * height * span,
            bytes_accessed=4 * height * span, transcendentals=0),
        name="turned_grad",
    )(*lefts, *rights)


def norm_rows(values, gain):
    return values * lax.rsqrt(jnp.mean(values * values, axis=-1, keepdims=True) + 1e-06) * gain


def norm_back(grad, values, gain):
    scale = lax.rsqrt(jnp.mean(values * values, axis=-1, keepdims=True) + 1e-06)
    unit = values * scale
    inner = grad * gain
    back = scale * (inner - unit * jnp.mean(inner * unit, axis=-1, keepdims=True))
    return back, jnp.sum(grad * unit, axis=0)


def dot(equation, left, right):
    return jnp.einsum(equation, left, right, preferred_element_type=f32)


def after(value, *others):
    return lax.optimization_barrier((value, *others))[0]


def per_device(shards, hidden_in, norm1_gain, qkv_weight, beta_weight, conv_weight, out_gain,
               out_weight, norm2_gain, gate_up_weight, down_weight, block_segments, cotangent):
    segments = block_segments[0]
    blocks = segments.shape[0]
    rows, model = hidden_in.shape
    length = rows * shards
    me = lax.axis_index("head")
    mine_z = lax.axis_index("z")

    def exchange(parts):
        return [parts[0]] + [
            lax.ppermute(parts[k], "head", [(i, i ^ k) for i in range(shards)])
            for k in range(1, shards)
        ]

    def gather_rows(own):
        return exchange([own] * shards)

    def scatter_sum(product):
        pieces = exchange([product[k * rows:(k + 1) * rows] for k in range(shards)])
        total = pieces[0].astype(f32)
        for piece in pieces[1:]:
            total = total + piece.astype(f32)
        return total

    keep = jnp.concatenate([jnp.zeros((1,), bool), segments[1:] == segments[:-1]])
    info = jnp.concatenate([me[None], keep]).astype(jnp.int32)
    taps = conv_weight.astype(f32).reshape(-1, conv_weight.shape[2])
    taps = jnp.pad(taps, ((0, 16 - taps.shape[0]), (0, 0)))
    gain = out_gain[None]

    hidden_parts = gather_rows(hidden_in)
    normed_all = jnp.concatenate(
        [norm_rows(part.astype(f32), norm1_gain).astype(bf16) for part in hidden_parts]
    )
    rows_in = hidden_in.astype(f32)
    cot_all = jnp.concatenate(gather_rows(cotangent))
    hidden_line = lax.all_gather(hidden_in, "z", axis=0)
    line = hidden_line.shape[0]
    cot_line = lax.all_gather(cot_all, "z", axis=0, tiled=True)

    projected = dot("td,sde->ste", normed_all, qkv_weight)
    beta_logit = dot("td,dh->th", normed_all, beta_weight)
    mixer_low, *saved = mixer_forward(info, projected, beta_logit, taps, gain, rows, shards, blocks)
    attn_rows = scatter_sum(after(dot("tc,cd->td", mixer_low, out_weight).astype(bf16), hidden_line))
    middle = rows_in + attn_rows
    second_low = norm_rows(middle, norm2_gain).astype(bf16)
    second_all = jnp.concatenate(gather_rows(second_low))
    second_line = lax.all_gather(second_all, "z", axis=0, tiled=True)

    def feed_forward(second, cot):
        gate_up = dot("td,sdf->stf", second, gate_up_weight)
        sigmoid_gate = jax.nn.sigmoid(gate_up[0])
        silu_gate = gate_up[0] * sigmoid_gate
        hidden_low = (silu_gate * gate_up[1]).astype(bf16)
        hidden_grad = dot("td,fd->tf", cot, down_weight)
        gate_grad = hidden_grad * gate_up[1] * sigmoid_gate * (1.0 + gate_up[0] * (1.0 - sigmoid_gate))
        up_grad = hidden_grad * silu_gate
        return hidden_low, jnp.stack([gate_grad, up_grad]).astype(bf16)

    hidden_low, gate_up_low = feed_forward(second_all, cot_all)
    second_grad = scatter_sum(dot("stf,sdf->td", gate_up_low, gate_up_weight).astype(bf16))
    ffn_rows = scatter_sum(dot("tf,fd->td", hidden_low, down_weight).astype(bf16))
    block_out = (middle + ffn_rows).astype(bf16)
    middle_part, norm2_gain_grad = norm_back(second_grad, middle, norm2_gain)
    middle_grad = cotangent.astype(f32) + middle_part
    attn_grad_all = jnp.concatenate(gather_rows(after(middle_grad.astype(bf16), cot_line)))
    mixer_in_grad = dot("td,cd->tc", attn_grad_all, out_weight)
    out_grad = dot("tc,td->cd", mixer_low, attn_grad_all).astype(bf16)
    mixer_in_grad = after(mixer_in_grad, out_grad)

    projected_low, beta_logit_grad, conv_grad, out_gain_grad = mixer_backward(
        info, mixer_in_grad, projected, beta_logit, taps, gain, saved, rows, shards, blocks
    )
    beta_low = beta_logit_grad[:, :beta_weight.shape[1]].astype(bf16)
    first_grad = scatter_sum(
        (dot("ste,sde->td", projected_low, qkv_weight) + dot("th,dh->td", beta_low, beta_weight)).astype(bf16)
    )
    rows_part, norm1_gain_grad = norm_back(first_grad, rows_in, norm1_gain)
    input_grad = middle_grad + rows_part
    projected_line = lax.all_gather(projected_low, "z", axis=1, tiled=True)
    beta_grad = dot("td,th->dh", normed_all, beta_low)

    def partner(value):
        return lax.ppermute(value, "core", [(0, 1), (1, 0)])

    cot_line = after(cot_line, projected_low)
    second_line = after(second_line, projected_low)
    hidden_every_low, gate_up_every = feed_forward(second_line, cot_line)
    out_grad = lax.psum(out_grad, ("z", "core"))
    gate_up_grad = planes_grad(
        [second_line, partner(second_line)], [gate_up_every, partner(gate_up_every)]
    )
    down_grad = turned_grad(
        [after(hidden_every_low, out_grad), partner(hidden_every_low)], [cot_line, partner(cot_line)]
    )
    out_grad = out_grad.astype(f32)
    hidden_every = jnp.stack(gather_rows(after(hidden_line, projected_low)))
    normed_every = norm_rows(hidden_every.astype(f32), norm1_gain).astype(bf16)
    normed_every = normed_every.transpose(1, 0, 2, 3).reshape(line * length, model)
    qkv_grad = pair_sum(
        [dot("td,te->de", normed_every, projected_line[s]).astype(bf16) for s in range(3)]
    )

    gains = jnp.concatenate([norm1_gain_grad, norm2_gain_grad, out_gain_grad[0]])
    small = jnp.concatenate([gains, beta_grad.T.reshape(-1), conv_grad[:12].reshape(-1)])
    small = small.reshape(-1, 128)

    def butterfly(value, axis, size):
        step = 1
        while step < size:
            value = value + lax.ppermute(value, axis, [(i, i ^ step) for i in range(size)])
            step *= 2
        return value

    small = butterfly(butterfly(small, "core", 2), "z", line).reshape(-1)
    gain_size = gains.size
    gains = butterfly(small[:gain_size].reshape(-1, 128), "head", shards).reshape(-1)
    beta_size = beta_grad.size
    beta_grad = small[gain_size:gain_size + beta_size].reshape(beta_grad.shape[::-1]).T
    conv_grad = small[gain_size + beta_size:].reshape(conv_weight.shape)
    return (
        block_out,
        input_grad,
        gains[:model],
        qkv_grad,
        beta_grad,
        conv_grad,
        gains[2 * model:],
        out_grad,
        gains[model:2 * model],
        gate_up_grad,
        down_grad,
    )


def solution(mesh):
    groups, shards = mesh.devices.shape
    split = Mesh(mesh.devices.reshape(groups // 2, 2, shards), ("z", "core", "head"))
    tokens = P(("z", "core", "head"), None)
    placed = (
        tokens,
        P(),
        P(None, None, "head"),
        P(None, "head"),
        P(None, None, "head"),
        P(),
        P("head", None),
        P(),
        P(None, None, "head"),
        P("head", None),
        P(("z", "core"), None),
        tokens,
    )
    return jax.shard_map(
        lambda *args: per_device(shards, *args),
        mesh=split,
        in_specs=placed,
        out_specs=(
            tokens,
            tokens,
            P(),
            P(None, None, "head"),
            P(None, "head"),
            P(None, None, "head"),
            P(),
            P("head", None),
            P(),
            P(None, None, "head"),
            P("head", None),
        ),
        check_vma=False,
    )
```

```python
import functools
import jax
import jax.numpy as jnp
from jax import lax
from jax.experimental import pallas as pl
from jax.experimental.pallas import tpu as pltpu
from jax.sharding import Mesh, PartitionSpec as P

f32 = jnp.float32
bf16 = jnp.bfloat16

DIMS = {"nn": (((1,), (0,)), ((), ())), "nt": (((1,), (1,)), ((), ())), "tn": (((0,), (0,)), ((), ()))}


def mm(left, right, form="nn"):
    return lax.dot_general(left.astype(bf16), right.astype(bf16), DIMS[form], preferred_element_type=f32)


def halves(value):
    high = value.astype(bf16)
    return high, (value - high.astype(f32)).astype(bf16)


def mm3(left, right, form="nn"):
    lh, ll = halves(left)
    rh, rl = halves(right)
    return mm(lh, rh, form) + (mm(lh, rl, form) + mm(ll, rh, form))


def sigmoid(value):
    return 1.0 / (1.0 + jnp.exp(-value))


def block_masks(length, size):
    row = lax.broadcasted_iota(jnp.int32, (length, length), 0)
    col = lax.broadcasted_iota(jnp.int32, (length, length), 1)
    same = (row ^ col) < size
    return (same & (row > col)), (same & (row >= col))


def keep_rows(info_ref, length, size):
    row = lax.broadcasted_iota(jnp.int32, (length, 1), 0)
    keep = jnp.zeros((length, 1), f32)
    for b in range(length // size):
        keep = jnp.where((row >= b * size) & (row < (b + 1) * size), info_ref[1 + b].astype(f32), keep)
    within = row & (size - 1)
    return [None] + [jnp.where(within >= shift, 1.0, keep) for shift in range(1, 4)]


def taken(ref, lead, me, rows, shards, cols):
    parts = []
    for j in range(shards):
        at = pl.ds(pl.multiple_of((me ^ j) * rows, rows), rows)
        parts.append(ref[lead + (at, cols)] if lead is not None else ref[at, cols])
    return jnp.concatenate(parts, 0)


def put(ref, lead, me, rows, shards, cols, value):
    for j in range(shards):
        at = pl.ds(pl.multiple_of((me ^ j) * rows, rows), rows)
        ref[lead + (at, cols)] = value[j * rows:(j + 1) * rows].astype(ref.dtype)


def forward_kernel(rows, shards, blocks, info_ref, proj_ref, logit_ref, taps_ref, gain_ref,
                   mixed_ref, conv_ref, o_ref, fresh_ref, state_ref, inv_ref,
                   q_s, k_s, u_s, w_s):
    length = rows * shards
    size = length // blocks
    heads = logit_ref.shape[1]
    width = proj_ref.shape[2] // heads
    me = info_ref[0]
    masks = keep_rows(info_ref, length, size)
    strict, inclusive = block_masks(length, size)
    logit = taken(logit_ref, (), me, rows, shards, slice(None))
    beta_all = sigmoid(logit)
    for h in range(heads):
        cols = slice(h * width, (h + 1) * width)
        beta = beta_all[:, h:h + 1]
        acts = []
        for s in range(3):
            x = taken(proj_ref, (s,), me, rows, shards, cols)
            z = x * taps_ref[4 * s:4 * s + 1, cols]
            for j in range(1, 4):
                z = z + pltpu.roll(x, j, 0) * (taps_ref[4 * s + j:4 * s + j + 1, cols] * masks[j])
            conv_ref[s, :, cols] = z
            acts.append(z * sigmoid(z))
        q0, k0, v = acts
        q = q0 * (lax.rsqrt(jnp.sum(q0 * q0, axis=-1, keepdims=True) + 1e-06) * width ** -0.5)
        k = k0 * lax.rsqrt(jnp.sum(k0 * k0, axis=-1, keepdims=True) + 1e-06)
        q_s[:, cols] = q
        k_s[:, cols] = k
        power = jnp.where(strict, mm3(k * -beta, k, "nt"), 0.0)
        inverse = power
        step = 1
        while 2 * step < size:
            power = mm3(power, power)
            inverse = inverse + power + mm3(inverse, power)
            step *= 2
        inv_ref[h] = inverse
        bk, bv = beta * k, beta * v
        w_s[:, cols] = bk + mm(inverse, bk)
        u_s[:, cols] = bv + mm(inverse, bv)
    states = [jnp.zeros((width, width), f32)] * heads
    for b in range(blocks):
        at = slice(b * size, (b + 1) * size)
        keep = info_ref[1 + b].astype(f32)
        for h in range(heads):
            cols = slice(h * width, (h + 1) * width)
            state = states[h] * keep
            state_ref[h, b] = state
            fresh = u_s[at, cols] - mm(w_s[at, cols], state)
            fresh_ref[at, cols] = fresh
            states[h] = state + mm(k_s[at, cols], fresh, "tn")
            o_ref[at, cols] = mm(q_s[at, cols], state)
    for h in range(heads):
        cols = slice(h * width, (h + 1) * width)
        scores = jnp.where(inclusive, mm(q_s[:, cols], k_s[:, cols], "nt"), 0.0)
        o = o_ref[:, cols] + mm(scores, fresh_ref[:, cols])
        o_ref[:, cols] = o
        mixed = o * lax.rsqrt(jnp.mean(o * o, axis=-1, keepdims=True) + 1e-05) * gain_ref[0:1, :]
        put(mixed_ref, (), me, rows, shards, cols, mixed)


def backward_kernel(rows, shards, blocks, info_ref, grad_ref, proj_ref, logit_ref, taps_ref, gain_ref,
                    conv_ref, o_ref, fresh_ref, state_ref, inv_ref,
                    proj_grad_ref, logit_grad_ref, taps_grad_ref, gain_grad_ref,
                    q_s, k_s, w_s, do_s, df_s, dq_s, dk_s):
    length = rows * shards
    size = length // blocks
    heads = logit_ref.shape[1]
    width = proj_ref.shape[2] // heads
    me = info_ref[0]
    masks = keep_rows(info_ref, length, size)
    strict, inclusive = block_masks(length, size)
    logit = taken(logit_ref, (), me, rows, shards, slice(None))
    beta_all = sigmoid(logit)
    gain_total = jnp.zeros((1, width), f32)
    lane = lax.broadcasted_iota(jnp.int32, (length, logit_grad_ref.shape[1]), 1)
    logit_grad = jnp.zeros((length, logit_grad_ref.shape[1]), f32)
    for h in range(heads):
        cols = slice(h * width, (h + 1) * width)
        beta = beta_all[:, h:h + 1]
        zq, zk = conv_ref[0, :, cols], conv_ref[1, :, cols]
        q0, k0 = zq * sigmoid(zq), zk * sigmoid(zk)
        q = q0 * (lax.rsqrt(jnp.sum(q0 * q0, axis=-1, keepdims=True) + 1e-06) * width ** -0.5)
        k = k0 * lax.rsqrt(jnp.sum(k0 * k0, axis=-1, keepdims=True) + 1e-06)
        q_s[:, cols] = q
        k_s[:, cols] = k
        bk = beta * k
        w_s[:, cols] = bk + mm(inv_ref[h], bk)
        g = taken(grad_ref, (), me, rows, shards, cols)
        o = o_ref[:, cols]
        r = lax.rsqrt(jnp.mean(o * o, axis=-1, keepdims=True) + 1e-05)
        on = o * r
        gain_total = gain_total + jnp.sum(g * on, axis=0, keepdims=True)
        dn = g * gain_ref[0:1, :]
        do = r * (dn - on * jnp.mean(dn * on, axis=-1, keepdims=True))
        do_s[:, cols] = do
        scores = jnp.where(inclusive, mm(q, k, "nt"), 0.0)
        df_s[:, cols] = mm(scores, do, "tn")
        dscores = jnp.where(inclusive, mm(do, fresh_ref[:, cols], "nt"), 0.0)
        dq_s[:, cols] = mm(dscores, k)
        dk_s[:, cols] = mm(dscores, q, "tn")
    gain_grad_ref[...] = jnp.broadcast_to(gain_total, gain_grad_ref.shape)
    carried = [jnp.zeros((width, width), f32)] * heads
    for b in reversed(range(blocks)):
        at = slice(b * size, (b + 1) * size)
        keep = info_ref[1 + b].astype(f32)
        for h in range(heads):
            cols = slice(h * width, (h + 1) * width)
            after = carried[h]
            df = df_s[at, cols] + mm(k_s[at, cols], after)
            df_s[at, cols] = df
            do = do_s[at, cols]
            carried[h] = keep * (after + mm(q_s[at, cols], do, "tn") - mm(w_s[at, cols], df, "tn"))
            dq_s[at, cols] = dq_s[at, cols] + mm(do, state_ref[h, b], "nt")
            dk_s[at, cols] = dk_s[at, cols] + mm(fresh_ref[at, cols], after, "nt")
    for h in range(heads):
        cols = slice(h * width, (h + 1) * width)
        beta = beta_all[:, h:h + 1]
        k = k_s[:, cols]
        df = df_s[:, cols]
        dr = df + mm(inv_ref[h], df, "tn")
        bdr = beta * dr
        fresh = fresh_ref[:, cols]
        lower = jnp.where(strict, mm(dr, fresh, "nt"), 0.0)
        blower = beta * lower
        zv = conv_ref[2, :, cols]
        sv = sigmoid(zv)
        held, back = [], []
        for b in range(blocks):
            at = slice(b * size, (b + 1) * size)
            held.append(mm(k[at], state_ref[h, b]))
            back.append(mm(bdr[at], state_ref[h, b], "nt"))
        excess = zv * sv - jnp.concatenate(held, 0)
        gram = mm(k, k, "nt")
        dbeta = jnp.sum(dr * excess, axis=-1, keepdims=True) - jnp.sum(lower * gram, axis=-1, keepdims=True)
        logit_grad = jnp.where(lane == h, dbeta * beta * (1.0 - beta), logit_grad)
        dk = dk_s[:, cols] - jnp.concatenate(back, 0) - (mm(blower, k) + mm(blower, k, "tn"))
        dq = dq_s[:, cols]
        for s, dy in ((0, dq), (1, dk), (2, bdr)):
            z = conv_ref[s, :, cols]
            sz = sigmoid(z)
            if s < 2:
                y = z * sz
                r = lax.rsqrt(jnp.sum(y * y, axis=-1, keepdims=True) + 1e-06)
                yn = y * r
                if s == 0:
                    r = r * width ** -0.5
                dy = r * (dy - yn * jnp.sum(dy * yn, axis=-1, keepdims=True))
            dz = dy * sz * (1.0 + z * (1.0 - sz))
            x = taken(proj_ref, (s,), me, rows, shards, cols)
            dx = dz * taps_ref[4 * s:4 * s + 1, cols]
            taps_grad_ref[4 * s:4 * s + 1, cols] = jnp.sum(dz * x, axis=0, keepdims=True)
            for j in range(1, 4):
                moved = dz * masks[j]
                taps_grad_ref[4 * s + j:4 * s + j + 1, cols] = jnp.sum(moved * pltpu.roll(x, j, 0), axis=0, keepdims=True)
                dx = dx + pltpu.roll(moved, length - j, 0) * taps_ref[4 * s + j:4 * s + j + 1, cols]
            put(proj_grad_ref, (s,), me, rows, shards, cols, dx)
    put(logit_grad_ref, (), me, rows, shards, slice(None), logit_grad)


SMEM = pl.BlockSpec(memory_space=pltpu.SMEM)
VMEM = pl.BlockSpec(memory_space=pltpu.VMEM)


def mixer_forward(info, projected, logit, taps, gain, rows, shards, blocks):
    _, length, span = projected.shape
    heads = logit.shape[1]
    width = span // heads
    shape = jax.ShapeDtypeStruct
    return pl.pallas_call(
        functools.partial(forward_kernel, rows, shards, blocks),
        out_shape=(
            shape((length, span), bf16),
            shape((3, length, span), f32),
            shape((length, span), f32),
            shape((length, span), f32),
            shape((heads, blocks, width, width), f32),
            shape((heads, length, length), f32),
        ),
        in_specs=[SMEM] + [VMEM] * 4,
        out_specs=(VMEM,) * 6,
        scratch_shapes=[pltpu.VMEM((length, span), f32)] * 4,
        compiler_params=pltpu.CompilerParams(vmem_limit_bytes=48 * 1024 * 1024),
        cost_estimate=pl.CostEstimate(flops=10**10, bytes_accessed=10 * 2**20, transcendentals=10**6),
        name="mixer_forward",
    )(info, projected, logit, taps, gain)


def mixer_backward(info, grad, projected, logit, taps, gain, saved, rows, shards, blocks):
    _, length, span = projected.shape
    heads = logit.shape[1]
    width = span // heads
    shape = jax.ShapeDtypeStruct
    return pl.pallas_call(
        functools.partial(backward_kernel, rows, shards, blocks),
        out_shape=(
            shape((3, length, span), bf16),
            shape((length, 128), f32),
            shape((16, span), f32),
            shape((8, width), f32),
        ),
        in_specs=[SMEM] + [VMEM] * 10,
        out_specs=(VMEM,) * 4,
        scratch_shapes=[pltpu.VMEM((length, span), f32)] * 7,
        compiler_params=pltpu.CompilerParams(vmem_limit_bytes=48 * 1024 * 1024),
        cost_estimate=pl.CostEstimate(flops=2 * 10**10, bytes_accessed=14 * 2**20, transcendentals=10**6),
        name="mixer_backward",
    )(info, grad, projected, logit, taps, gain, *saved)


def rows_kernel(second_ref, cot_ref, gate_up_ref, down_ref, out_ref, gate_s, up_s, grad_s):
    step = pl.program_id(0)
    second = second_ref[...]
    cot = cot_ref[...]
    cot = cot.reshape(-1, cot.shape[-1])
    gate = jnp.dot(second, gate_up_ref[0], preferred_element_type=f32)
    up = jnp.dot(second, gate_up_ref[1], preferred_element_type=f32)
    grad = lax.dot_general(cot, down_ref[...], DIMS["nt"], preferred_element_type=f32)

    @pl.when(step == 0)
    def _():
        gate_s[...] = gate
        up_s[...] = up
        grad_s[...] = grad

    @pl.when(step > 0)
    def _():
        gate_s[...] += gate
        up_s[...] += up
        grad_s[...] += grad

    @pl.when(step == pl.num_programs(0) - 1)
    def _():
        chunk = 32

        def body(r, carry):
            at = pl.ds(pl.multiple_of(r * chunk, chunk), chunk)
            gate, up, grad = gate_s[at], up_s[at], grad_s[at]
            sg = sigmoid(gate)
            silu = gate * sg
            out_ref[0, at] = (grad * up * sg * (1.0 + gate * (1.0 - sg))).astype(bf16)
            out_ref[1, at] = (grad * silu).astype(bf16)
            out_ref[2, at] = (silu * up).astype(bf16)
            return carry

        lax.fori_loop(0, gate_s.shape[0] // chunk, body, 0)


def feed_forward_rows(second, cot, part, gate_up_weight, down_weight, tile=512):
    length, model = second.shape
    line, _, rows, _ = cot.shape
    hidden = down_weight.shape[0]
    return pl.pallas_call(
        rows_kernel,
        grid=(model // tile,),
        in_specs=[
            pl.BlockSpec((length, tile), lambda i: (0, i)),
            pl.BlockSpec((line, None, rows, tile), lambda i: (0, part, 0, i)),
            pl.BlockSpec((2, tile, hidden), lambda i: (0, i, 0)),
            pl.BlockSpec((hidden, tile), lambda i: (0, i)),
        ],
        out_specs=pl.BlockSpec((3, length, hidden), lambda i: (0, 0, 0), pipeline_mode=pl.Buffered(1)),
        out_shape=jax.ShapeDtypeStruct((3, length, hidden), bf16),
        scratch_shapes=[pltpu.VMEM((length, hidden), f32)] * 3,
        compiler_params=pltpu.CompilerParams(vmem_limit_bytes=56 * 1024 * 1024),
        cost_estimate=pl.CostEstimate(
            flops=6 * length * model * hidden, bytes_accessed=6 * model * hidden, transcendentals=length * hidden),
        name="feed_forward_rows",
    )(second, cot, gate_up_weight, down_weight)


def swap(value):
    return lax.ppermute(value, "core", [(0, 1), (1, 0)])


def planes_kernel(pieces, core_ref, *refs):
    out_ref, sent_ref = refs[2 * pieces:]
    lefts = [refs[p][...].T for p in range(pieces)]
    for s in range(out_ref.shape[0]):
        total = None
        for p in range(pieces):
            term = jnp.dot(lefts[p], refs[pieces + p][s], preferred_element_type=f32)
            total = term if total is None else total + term
        low = total.astype(bf16)
        sent_ref[s] = low
        out_ref[s] = low.astype(f32)


def planes_fill(core_ref, whole_ref, part_ref, out_ref):
    out_ref[...] = part_ref[...].astype(f32)


def planes_grad(core, lefts, rights, planes, tile=256):
    pieces = len(lefts)
    height = lefts[0].shape[1]
    _, depth, span = rights[0].shape
    steps = height // 2 // tile
    whole = jax.ShapeDtypeStruct((planes, height, span), f32)
    params = pltpu.CompilerParams(vmem_limit_bytes=48 * 1024 * 1024)
    own, sent = pl.pallas_call(
        functools.partial(planes_kernel, pieces),
        grid_spec=pltpu.PrefetchScalarGridSpec(
            num_scalar_prefetch=1,
            grid=(steps,),
            in_specs=[pl.BlockSpec((depth, tile), lambda i, c: (0, c[0] * steps + i))] * pieces
            + [pl.BlockSpec((planes, depth, span), lambda i, c: (0, 0, 0), pipeline_mode=pl.Buffered(1))] * pieces,
            out_specs=(
                pl.BlockSpec((planes, tile, span), lambda i, c: (0, c[0] * steps + i, 0)),
                pl.BlockSpec((planes, tile, span), lambda i, c: (0, i, 0)),
            ),
        ),
        out_shape=(whole, jax.ShapeDtypeStruct((planes, height // 2, span), bf16)),
        compiler_params=params,
        cost_estimate=pl.CostEstimate(
            flops=pieces * depth * planes * height * span // 4,
            bytes_accessed=planes * height * span, transcendentals=0),
        name="planes_grad",
    )(core, *lefts, *rights)

    def finish(part):
        return pl.pallas_call(
            planes_fill,
            grid_spec=pltpu.PrefetchScalarGridSpec(
                num_scalar_prefetch=1,
                grid=(planes, steps),
                in_specs=[
                    pl.BlockSpec(memory_space=pl.ANY),
                    pl.BlockSpec((1, tile, span), lambda s, i, c: (s, i, 0)),
                ],
                out_specs=pl.BlockSpec((1, tile, span), lambda s, i, c: (s, (1 - c[0]) * steps + i, 0)),
            ),
            out_shape=whole,
            input_output_aliases={1: 0},
            compiler_params=params,
            cost_estimate=pl.CostEstimate(
                flops=planes * height * span // 2, bytes_accessed=3 * planes * height * span, transcendentals=0),
            name="planes_fill",
        )(core, own, part)

    return sent, finish


def turned_kernel(pieces, core_ref, *refs):
    out_ref, sent_ref = refs[2 * pieces:2 * pieces + 2]
    turned = refs[2 * pieces + 2:]

    @pl.when(pl.program_id(0) == 0)
    def _():
        for p in range(pieces):
            turned[p][...] = refs[p][...].T

    total = None
    for p in range(pieces):
        right = refs[pieces + p][...]
        right = right.reshape(-1, right.shape[-1])
        term = jnp.dot(turned[p][...], right, preferred_element_type=f32)
        total = term if total is None else total + term
    low = total.astype(bf16)
    sent_ref[...] = low
    out_ref[...] = low.astype(f32)


def turned_grad(core, lefts, rights, tile=256):
    pieces = len(lefts)
    _, depth, height = lefts[0].shape
    line, parts, rows, span = rights[0].shape

    def right_spec(h):
        return pl.BlockSpec((line, None, rows, tile), lambda i, c: (0, h, 0, c[0] * steps + i))

    steps = span // 2 // tile
    whole = jax.ShapeDtypeStruct((height, span), f32)
    params = pltpu.CompilerParams(vmem_limit_bytes=48 * 1024 * 1024)
    own, sent = pl.pallas_call(
        functools.partial(turned_kernel, pieces),
        grid_spec=pltpu.PrefetchScalarGridSpec(
            num_scalar_prefetch=1,
            grid=(steps,),
            in_specs=[pl.BlockSpec((None, depth, height), lambda i, c: (2, 0, 0), pipeline_mode=pl.Buffered(1))] * pieces
            + [right_spec(p % parts) for p in range(pieces)],
            out_specs=(
                pl.BlockSpec((height, tile), lambda i, c: (0, c[0] * steps + i)),
                pl.BlockSpec((height, tile), lambda i, c: (0, i)),
            ),
            scratch_shapes=[pltpu.VMEM((height, depth), bf16)] * pieces,
        ),
        out_shape=(whole, jax.ShapeDtypeStruct((height, span // 2), bf16)),
        compiler_params=params,
        cost_estimate=pl.CostEstimate(
            flops=pieces * depth * height * span // 4,
            bytes_accessed=height * span, transcendentals=0),
        name="turned_grad",
    )(core, *lefts, *[right for right in rights for _ in range(parts)])

    def finish(part):
        return pl.pallas_call(
            planes_fill,
            grid_spec=pltpu.PrefetchScalarGridSpec(
                num_scalar_prefetch=1,
                grid=(steps,),
                in_specs=[
                    pl.BlockSpec(memory_space=pl.ANY),
                    pl.BlockSpec((height, tile), lambda i, c: (0, i)),
                ],
                out_specs=pl.BlockSpec((height, tile), lambda i, c: (0, (1 - c[0]) * steps + i)),
            ),
            out_shape=whole,
            input_output_aliases={1: 0},
            compiler_params=params,
            cost_estimate=pl.CostEstimate(
                flops=height * span // 2, bytes_accessed=3 * height * span, transcendentals=0),
            name="turned_fill",
        )(core, own, part)

    return sent, finish


def norm_rows(values, gain):
    return values * lax.rsqrt(jnp.mean(values * values, axis=-1, keepdims=True) + 1e-06) * gain


def norm_back(grad, values, gain):
    scale = lax.rsqrt(jnp.mean(values * values, axis=-1, keepdims=True) + 1e-06)
    unit = values * scale
    inner = grad * gain
    back = scale * (inner - unit * jnp.mean(inner * unit, axis=-1, keepdims=True))
    return back, jnp.sum(grad * unit, axis=0)


def dot(equation, left, right):
    return jnp.einsum(equation, left, right, preferred_element_type=f32)


def after(value, *others):
    return lax.optimization_barrier((value, *others))[0]


def per_device(shards, hidden_in, norm1_gain, qkv_weight, beta_weight, conv_weight, out_gain,
               out_weight, norm2_gain, gate_up_weight, down_weight, block_segments, cotangent):
    segments = block_segments[0]
    blocks = segments.shape[0]
    rows, model = hidden_in.shape
    length = rows * shards
    me = lax.axis_index("head")
    mine_z = lax.axis_index("z")

    half = shards // 2

    def exchange(parts):
        return [parts[0]] + [
            lax.ppermute(parts[k], "head", [(i, i ^ k) for i in range(shards)])
            for k in range(1, shards)
        ]

    def move(value, k):
        return lax.ppermute(value, "head", [(i, i ^ k) for i in range(shards)])

    def relay(pieces):
        far = []
        for k in range(half + 1, shards):
            via = k ^ half
            cut = pieces[0].shape[0] // 2
            far.append(jnp.concatenate([move(pieces[half][:cut], via), move(pieces[via][cut:], half)]))
        return far

    def gather_rows(own):
        return exchange([own] * shards)

    def scatter_sum(product):
        pieces = exchange([product[k * rows:(k + 1) * rows] for k in range(shards)])
        total = pieces[0].astype(f32)
        for piece in pieces[1:]:
            total = total + piece.astype(f32)
        return total

    keep = jnp.concatenate([jnp.zeros((1,), bool), segments[1:] == segments[:-1]])
    info = jnp.concatenate([me[None], keep]).astype(jnp.int32)
    taps = conv_weight.astype(f32).reshape(-1, conv_weight.shape[2])
    taps = jnp.pad(taps, ((0, 16 - taps.shape[0]), (0, 0)))
    gain = out_gain[None]

    core = lax.axis_index("core")
    hidden_parts = gather_rows(hidden_in)
    normed_all = jnp.concatenate(
        [norm_rows(part.astype(f32), norm1_gain).astype(bf16) for part in hidden_parts]
    )
    rows_in = hidden_in.astype(f32)
    hidden_line = lax.all_gather(hidden_in, "z", axis=0)
    line = hidden_line.shape[0]
    projected = dot("td,sde->ste", normed_all, qkv_weight)
    cot_all = jnp.concatenate([after(part, projected) for part in gather_rows(cotangent)])
    cot_line = lax.all_gather(cot_all, "z", axis=0)
    beta_logit = dot("td,dh->th", normed_all, beta_weight)
    mixer_low, *saved = mixer_forward(
        info, after(projected, cot_all), beta_logit, taps, gain, rows, shards, blocks
    )
    attn_rows = scatter_sum(after(dot("tc,cd->td", mixer_low, out_weight).astype(bf16), hidden_line))
    middle = rows_in + attn_rows
    second_low = norm_rows(middle, norm2_gain).astype(bf16)
    second_all = jnp.concatenate(gather_rows(second_low))
    second_line = lax.all_gather(after(second_low, cot_line), "z", axis=0)
    hidden_ready = after(hidden_line, second_all)
    hidden_near = [move(hidden_ready, k) for k in range(1, half + 1)]

    def feed_forward(second, cot):
        gate_up = dot("td,sdf->stf", second, gate_up_weight)
        sigmoid_gate = jax.nn.sigmoid(gate_up[0])
        silu_gate = gate_up[0] * sigmoid_gate
        hidden_low = (silu_gate * gate_up[1]).astype(bf16)
        hidden_grad = dot("td,fd->tf", cot, down_weight)
        gate_grad = hidden_grad * gate_up[1] * sigmoid_gate * (1.0 + gate_up[0] * (1.0 - sigmoid_gate))
        up_grad = hidden_grad * silu_gate
        return hidden_low, jnp.stack([gate_grad, up_grad]).astype(bf16)

    hidden_low, gate_up_low = feed_forward(second_all, cot_all)
    second_grad = scatter_sum(after(dot("stf,sdf->td", gate_up_low, gate_up_weight).astype(bf16), *hidden_near))
    ffn_product = dot("tf,fd->td", hidden_low, down_weight).astype(bf16)
    middle_part, norm2_gain_grad = norm_back(after(second_grad, cot_line, ffn_product), middle, norm2_gain)
    middle_grad = cotangent.astype(f32) + middle_part
    attn_grad_all = jnp.concatenate(gather_rows(middle_grad.astype(bf16)))
    mixer_in_grad = dot("td,cd->tc", attn_grad_all, out_weight)

    projected_low, beta_logit_grad, conv_grad, out_gain_grad = mixer_backward(
        info, mixer_in_grad, projected, beta_logit, taps, gain, saved, rows, shards, blocks
    )
    projected_line = lax.all_gather(projected_low, "z", axis=1, tiled=True)
    second_ready = after(second_line, projected_low)
    second_parts = [second_ready] + [move(second_ready, k) for k in range(1, half + 1)]
    beta_low = beta_logit_grad[:, :beta_weight.shape[1]].astype(bf16)
    first_product = dot("ste,sde->td", projected_low, qkv_weight) + dot("th,dh->td", beta_low, beta_weight)
    beta_grad = dot("td,th->dh", normed_all, beta_low)

    both = jnp.stack([first_product.astype(bf16), ffn_product]).reshape(2, shards, rows, model)

    out_partial = dot("tc,td->cd", mixer_low, attn_grad_all).astype(bf16)
    span = out_partial.shape[0] // 2
    out_half = lax.dynamic_slice_in_dim(out_partial, core * span, span).astype(f32)
    out_half = out_half + swap(lax.dynamic_slice_in_dim(out_partial, (1 - core) * span, span)).astype(f32)
    out_half = out_half.astype(bf16)

    cot_other = swap(cot_line)
    cot_line = cot_line.reshape(line, 2, half * rows, model)
    second_lines, line_rows, others = [], [], []
    second_parts = second_parts + relay(second_parts)
    hidden_near = [after(piece, second_parts[half]) for piece in hidden_near]
    hidden_far = relay([hidden_line, *hidden_near])
    for h in range(2):
        pieces = second_parts[h * half:(h + 1) * half]
        if h == 1:
            pieces = [after(piece, line_rows[0], out_half) for piece in pieces]
        piece = jnp.stack(pieces, 1).reshape(line * half * rows, model)
        if h == 0:
            piece = after(piece, both, cot_other, second_parts[half])
        else:
            piece = after(piece, *hidden_far, *others)
        second_lines.append(piece)
        others.append(swap(piece))
        line_rows.append(feed_forward_rows(piece, cot_line, h, gate_up_weight, down_weight))
    out_every = lax.all_gather(after(out_half, line_rows[0]), "z", axis=0)
    hidden_every = jnp.stack([hidden_line, *hidden_near, *hidden_far])
    row_others = [swap(part) for part in line_rows]
    down_part, down_finish = turned_grad(
        core[None], [after(line_rows[0], row_others[0], projected_line, *others), line_rows[1], *row_others],
        [cot_line, cot_other.reshape(cot_line.shape)],
    )
    normed_every = norm_rows(hidden_every.astype(f32), norm1_gain).astype(bf16)
    normed_every = normed_every.transpose(1, 0, 2, 3).reshape(line * length, model)

    both_parts = after(both, line_rows[1])
    first_grad, ffn_rows = sum(
        piece.astype(f32) for piece in exchange([both_parts[:, k] for k in range(shards)])
    )
    first_grad = after(first_grad, down_part)
    block_out = (middle + ffn_rows).astype(bf16)
    rows_part, norm1_gain_grad = norm_back(first_grad, rows_in, norm1_gain)
    input_grad = middle_grad + rows_part
    gains = jnp.concatenate([norm1_gain_grad, norm2_gain_grad, out_gain_grad[0]])
    small = jnp.concatenate([gains, beta_grad.T.reshape(-1), conv_grad[:12].reshape(-1)]).reshape(-1, 128)

    def total(value, axis, size):
        values = [value] + [
            lax.ppermute(value, axis, [(i, i ^ k) for i in range(size)]) for k in range(1, size)
        ]
        while len(values) > 1:
            values = [left + right for left, right in zip(values[::2], values[1::2])]
        return values[0]

    gate_up_part, gate_up_finish = planes_grad(
        core[None], [after(second_lines[0], normed_every, down_part), second_lines[1], *others],
        [*line_rows, *row_others], 2,
    )
    small = total(small, "core", 2)
    qkv_part, qkv_finish = planes_grad(
        core[None], [after(normed_every, small, gate_up_part), swap(normed_every)],
        [projected_line, swap(projected_line)], 3,
    )
    down_grad = down_finish(after(swap(down_part), qkv_part, out_every))
    small = total(small, "z", line)
    small = small.reshape(-1)
    gain_size = gains.size
    gains = total(small[:gain_size].reshape(-1, 128), "head", shards).reshape(-1)
    out_rows = jnp.sum(out_every.astype(f32), axis=0).astype(bf16)
    out_other = swap(out_rows)
    out_grad = jnp.where(
        core == 0, jnp.concatenate([out_rows, out_other]), jnp.concatenate([out_other, out_rows])
    ).astype(f32)
    gate_up_grad = gate_up_finish(after(swap(gate_up_part), down_grad, small))
    qkv_grad = qkv_finish(after(swap(qkv_part), gate_up_grad))
    beta_size = beta_grad.size
    beta_grad = small[gain_size:gain_size + beta_size].reshape(beta_grad.shape[::-1]).T
    conv_grad = small[gain_size + beta_size:].reshape(conv_weight.shape)
    return (
        block_out,
        input_grad,
        gains[:model],
        qkv_grad,
        beta_grad,
        conv_grad,
        gains[2 * model:],
        out_grad,
        gains[model:2 * model],
        gate_up_grad,
        down_grad,
    )


def solution(mesh):
    groups, shards = mesh.devices.shape
    split = Mesh(mesh.devices.reshape(groups // 2, 2, shards), ("z", "core", "head"))
    tokens = P(("z", "core", "head"), None)
    placed = (
        tokens,
        P(),
        P(None, None, "head"),
        P(None, "head"),
        P(None, None, "head"),
        P(),
        P("head", None),
        P(),
        P(None, None, "head"),
        P("head", None),
        P(("z", "core"), None),
        tokens,
    )
    return jax.shard_map(
        lambda *args: per_device(shards, *args),
        mesh=split,
        in_specs=placed,
        out_specs=(
            tokens,
            tokens,
            P(),
            P(None, None, "head"),
            P(None, "head"),
            P(None, None, "head"),
            P(),
            P("head", None),
            P(),
            P(None, None, "head"),
            P("head", None),
        ),
        check_vma=False,
    )
```

```python
import functools
import jax
import jax.numpy as jnp
from jax import lax
from jax.experimental import pallas as pl
from jax.experimental.pallas import tpu as pltpu
from jax.sharding import Mesh, PartitionSpec as P

f32 = jnp.float32
bf16 = jnp.bfloat16

DIMS = {"nn": (((1,), (0,)), ((), ())), "nt": (((1,), (1,)), ((), ())), "tn": (((0,), (0,)), ((), ()))}


def mm(left, right, form="nn"):
    return lax.dot_general(left.astype(bf16), right.astype(bf16), DIMS[form], preferred_element_type=f32)


def halves(value):
    high = value.astype(bf16)
    return high, (value - high.astype(f32)).astype(bf16)


def mm3(left, right, form="nn"):
    lh, ll = halves(left)
    rh, rl = halves(right)
    return mm(lh, rh, form) + (mm(lh, rl, form) + mm(ll, rh, form))


def sigmoid(value):
    return 1.0 / (1.0 + jnp.exp(-value))


def block_masks(length, size):
    row = lax.broadcasted_iota(jnp.int32, (length, length), 0)
    col = lax.broadcasted_iota(jnp.int32, (length, length), 1)
    same = (row ^ col) < size
    return (same & (row > col)), (same & (row >= col))


def keep_rows(info_ref, length, size):
    row = lax.broadcasted_iota(jnp.int32, (length, 1), 0)
    keep = jnp.zeros((length, 1), f32)
    for b in range(length // size):
        keep = jnp.where((row >= b * size) & (row < (b + 1) * size), info_ref[1 + b].astype(f32), keep)
    within = row & (size - 1)
    return [None] + [jnp.where(within >= shift, 1.0, keep) for shift in range(1, 4)]


def taken(ref, lead, me, rows, shards, cols):
    parts = []
    for j in range(shards):
        at = pl.ds(pl.multiple_of((me ^ j) * rows, rows), rows)
        parts.append(ref[lead + (at, cols)] if lead is not None else ref[at, cols])
    return jnp.concatenate(parts, 0)


def put(ref, lead, me, rows, shards, cols, value):
    for j in range(shards):
        at = pl.ds(pl.multiple_of((me ^ j) * rows, rows), rows)
        ref[lead + (at, cols)] = value[j * rows:(j + 1) * rows].astype(ref.dtype)


def forward_kernel(rows, shards, blocks, info_ref, proj_ref, logit_ref, taps_ref, gain_ref,
                   mixed_ref, conv_ref, o_ref, fresh_ref, state_ref, inv_ref,
                   q_s, k_s, u_s, w_s):
    length = rows * shards
    size = length // blocks
    heads = logit_ref.shape[1]
    width = proj_ref.shape[2] // heads
    me = info_ref[0]
    masks = keep_rows(info_ref, length, size)
    strict, inclusive = block_masks(length, size)
    logit = taken(logit_ref, (), me, rows, shards, slice(None))
    beta_all = sigmoid(logit)
    for h in range(heads):
        cols = slice(h * width, (h + 1) * width)
        beta = beta_all[:, h:h + 1]
        acts = []
        for s in range(3):
            x = taken(proj_ref, (s,), me, rows, shards, cols)
            z = x * taps_ref[4 * s:4 * s + 1, cols]
            for j in range(1, 4):
                z = z + pltpu.roll(x, j, 0) * (taps_ref[4 * s + j:4 * s + j + 1, cols] * masks[j])
            conv_ref[s, :, cols] = z
            acts.append(z * sigmoid(z))
        q0, k0, v = acts
        q = q0 * (lax.rsqrt(jnp.sum(q0 * q0, axis=-1, keepdims=True) + 1e-06) * width ** -0.5)
        k = k0 * lax.rsqrt(jnp.sum(k0 * k0, axis=-1, keepdims=True) + 1e-06)
        q_s[:, cols] = q
        k_s[:, cols] = k
        power = jnp.where(strict, mm3(k * -beta, k, "nt"), 0.0)
        inverse = power
        step = 1
        while 2 * step < size:
            power = mm3(power, power)
            inverse = inverse + power + mm3(inverse, power)
            step *= 2
        inv_ref[h] = inverse
        bk, bv = beta * k, beta * v
        w_s[:, cols] = bk + mm(inverse, bk)
        u_s[:, cols] = bv + mm(inverse, bv)
    states = [jnp.zeros((width, width), f32)] * heads
    for b in range(blocks):
        at = slice(b * size, (b + 1) * size)
        keep = info_ref[1 + b].astype(f32)
        for h in range(heads):
            cols = slice(h * width, (h + 1) * width)
            state = states[h] * keep
            state_ref[h, b] = state
            fresh = u_s[at, cols] - mm(w_s[at, cols], state)
            fresh_ref[at, cols] = fresh
            states[h] = state + mm(k_s[at, cols], fresh, "tn")
            o_ref[at, cols] = mm(q_s[at, cols], state)
    for h in range(heads):
        cols = slice(h * width, (h + 1) * width)
        scores = jnp.where(inclusive, mm(q_s[:, cols], k_s[:, cols], "nt"), 0.0)
        o = o_ref[:, cols] + mm(scores, fresh_ref[:, cols])
        o_ref[:, cols] = o
        mixed = o * lax.rsqrt(jnp.mean(o * o, axis=-1, keepdims=True) + 1e-05) * gain_ref[0:1, :]
        put(mixed_ref, (), me, rows, shards, cols, mixed)


def backward_kernel(rows, shards, blocks, info_ref, grad_ref, proj_ref, logit_ref, taps_ref, gain_ref,
                    conv_ref, o_ref, fresh_ref, state_ref, inv_ref,
                    proj_grad_ref, logit_grad_ref, taps_grad_ref, gain_grad_ref,
                    q_s, k_s, w_s, do_s, df_s, dq_s, dk_s):
    length = rows * shards
    size = length // blocks
    heads = logit_ref.shape[1]
    width = proj_ref.shape[2] // heads
    me = info_ref[0]
    masks = keep_rows(info_ref, length, size)
    strict, inclusive = block_masks(length, size)
    logit = taken(logit_ref, (), me, rows, shards, slice(None))
    beta_all = sigmoid(logit)
    gain_total = jnp.zeros((1, width), f32)
    lane = lax.broadcasted_iota(jnp.int32, (length, logit_grad_ref.shape[1]), 1)
    logit_grad = jnp.zeros((length, logit_grad_ref.shape[1]), f32)
    for h in range(heads):
        cols = slice(h * width, (h + 1) * width)
        beta = beta_all[:, h:h + 1]
        zq, zk = conv_ref[0, :, cols], conv_ref[1, :, cols]
        q0, k0 = zq * sigmoid(zq), zk * sigmoid(zk)
        q = q0 * (lax.rsqrt(jnp.sum(q0 * q0, axis=-1, keepdims=True) + 1e-06) * width ** -0.5)
        k = k0 * lax.rsqrt(jnp.sum(k0 * k0, axis=-1, keepdims=True) + 1e-06)
        q_s[:, cols] = q
        k_s[:, cols] = k
        bk = beta * k
        w_s[:, cols] = bk + mm(inv_ref[h], bk)
        g = taken(grad_ref, (), me, rows, shards, cols)
        o = o_ref[:, cols]
        r = lax.rsqrt(jnp.mean(o * o, axis=-1, keepdims=True) + 1e-05)
        on = o * r
        gain_total = gain_total + jnp.sum(g * on, axis=0, keepdims=True)
        dn = g * gain_ref[0:1, :]
        do = r * (dn - on * jnp.mean(dn * on, axis=-1, keepdims=True))
        do_s[:, cols] = do
        scores = jnp.where(inclusive, mm(q, k, "nt"), 0.0)
        df_s[:, cols] = mm(scores, do, "tn")
        dscores = jnp.where(inclusive, mm(do, fresh_ref[:, cols], "nt"), 0.0)
        dq_s[:, cols] = mm(dscores, k)
        dk_s[:, cols] = mm(dscores, q, "tn")
    gain_grad_ref[...] = jnp.broadcast_to(gain_total, gain_grad_ref.shape)
    carried = [jnp.zeros((width, width), f32)] * heads
    for b in reversed(range(blocks)):
        at = slice(b * size, (b + 1) * size)
        keep = info_ref[1 + b].astype(f32)
        for h in range(heads):
            cols = slice(h * width, (h + 1) * width)
            after = carried[h]
            df = df_s[at, cols] + mm(k_s[at, cols], after)
            df_s[at, cols] = df
            do = do_s[at, cols]
            carried[h] = keep * (after + mm(q_s[at, cols], do, "tn") - mm(w_s[at, cols], df, "tn"))
            dq_s[at, cols] = dq_s[at, cols] + mm(do, state_ref[h, b], "nt")
            dk_s[at, cols] = dk_s[at, cols] + mm(fresh_ref[at, cols], after, "nt")
    for h in range(heads):
        cols = slice(h * width, (h + 1) * width)
        beta = beta_all[:, h:h + 1]
        k = k_s[:, cols]
        df = df_s[:, cols]
        dr = df + mm(inv_ref[h], df, "tn")
        bdr = beta * dr
        fresh = fresh_ref[:, cols]
        lower = jnp.where(strict, mm(dr, fresh, "nt"), 0.0)
        blower = beta * lower
        zv = conv_ref[2, :, cols]
        sv = sigmoid(zv)
        held, back = [], []
        for b in range(blocks):
            at = slice(b * size, (b + 1) * size)
            held.append(mm(k[at], state_ref[h, b]))
            back.append(mm(bdr[at], state_ref[h, b], "nt"))
        excess = zv * sv - jnp.concatenate(held, 0)
        gram = mm(k, k, "nt")
        dbeta = jnp.sum(dr * excess, axis=-1, keepdims=True) - jnp.sum(lower * gram, axis=-1, keepdims=True)
        logit_grad = jnp.where(lane == h, dbeta * beta * (1.0 - beta), logit_grad)
        dk = dk_s[:, cols] - jnp.concatenate(back, 0) - (mm(blower, k) + mm(blower, k, "tn"))
        dq = dq_s[:, cols]
        for s, dy in ((0, dq), (1, dk), (2, bdr)):
            z = conv_ref[s, :, cols]
            sz = sigmoid(z)
            if s < 2:
                y = z * sz
                r = lax.rsqrt(jnp.sum(y * y, axis=-1, keepdims=True) + 1e-06)
                yn = y * r
                if s == 0:
                    r = r * width ** -0.5
                dy = r * (dy - yn * jnp.sum(dy * yn, axis=-1, keepdims=True))
            dz = dy * sz * (1.0 + z * (1.0 - sz))
            x = taken(proj_ref, (s,), me, rows, shards, cols)
            dx = dz * taps_ref[4 * s:4 * s + 1, cols]
            taps_grad_ref[4 * s:4 * s + 1, cols] = jnp.sum(dz * x, axis=0, keepdims=True)
            for j in range(1, 4):
                moved = dz * masks[j]
                taps_grad_ref[4 * s + j:4 * s + j + 1, cols] = jnp.sum(moved * pltpu.roll(x, j, 0), axis=0, keepdims=True)
                dx = dx + pltpu.roll(moved, length - j, 0) * taps_ref[4 * s + j:4 * s + j + 1, cols]
            put(proj_grad_ref, (s,), me, rows, shards, cols, dx)
    put(logit_grad_ref, (), me, rows, shards, slice(None), logit_grad)


SMEM = pl.BlockSpec(memory_space=pltpu.SMEM)
VMEM = pl.BlockSpec(memory_space=pltpu.VMEM)


def mixer_forward(info, projected, logit, taps, gain, rows, shards, blocks):
    _, length, span = projected.shape
    heads = logit.shape[1]
    width = span // heads
    shape = jax.ShapeDtypeStruct
    return pl.pallas_call(
        functools.partial(forward_kernel, rows, shards, blocks),
        out_shape=(
            shape((length, span), bf16),
            shape((3, length, span), f32),
            shape((length, span), f32),
            shape((length, span), f32),
            shape((heads, blocks, width, width), f32),
            shape((heads, length, length), f32),
        ),
        in_specs=[SMEM] + [VMEM] * 4,
        out_specs=(VMEM,) * 6,
        scratch_shapes=[pltpu.VMEM((length, span), f32)] * 4,
        compiler_params=pltpu.CompilerParams(vmem_limit_bytes=48 * 1024 * 1024),
        cost_estimate=pl.CostEstimate(flops=10**10, bytes_accessed=10 * 2**20, transcendentals=10**6),
        name="mixer_forward",
    )(info, projected, logit, taps, gain)


def mixer_backward(info, grad, projected, logit, taps, gain, saved, rows, shards, blocks):
    _, length, span = projected.shape
    heads = logit.shape[1]
    width = span // heads
    shape = jax.ShapeDtypeStruct
    return pl.pallas_call(
        functools.partial(backward_kernel, rows, shards, blocks),
        out_shape=(
            shape((3, length, span), bf16),
            shape((length, 128), f32),
            shape((16, span), f32),
            shape((8, width), f32),
        ),
        in_specs=[SMEM] + [VMEM] * 10,
        out_specs=(VMEM,) * 4,
        scratch_shapes=[pltpu.VMEM((length, span), f32)] * 7,
        compiler_params=pltpu.CompilerParams(vmem_limit_bytes=48 * 1024 * 1024),
        cost_estimate=pl.CostEstimate(flops=2 * 10**10, bytes_accessed=14 * 2**20, transcendentals=10**6),
        name="mixer_backward",
    )(info, grad, projected, logit, taps, gain, *saved)


def rows_kernel(second_ref, cot_ref, gate_up_ref, down_ref, out_ref, gate_s, up_s, grad_s):
    step = pl.program_id(0)
    second = second_ref[...]
    cot = cot_ref[...]
    cot = cot.reshape(-1, cot.shape[-1])
    gate = jnp.dot(second, gate_up_ref[0], preferred_element_type=f32)
    up = jnp.dot(second, gate_up_ref[1], preferred_element_type=f32)
    grad = lax.dot_general(cot, down_ref[...], DIMS["nt"], preferred_element_type=f32)

    @pl.when(step == 0)
    def _():
        gate_s[...] = gate
        up_s[...] = up
        grad_s[...] = grad

    @pl.when(step > 0)
    def _():
        gate_s[...] += gate
        up_s[...] += up
        grad_s[...] += grad

    @pl.when(step == pl.num_programs(0) - 1)
    def _():
        chunk = 32

        def body(r, carry):
            at = pl.ds(pl.multiple_of(r * chunk, chunk), chunk)
            gate, up, grad = gate_s[at], up_s[at], grad_s[at]
            sg = sigmoid(gate)
            silu = gate * sg
            out_ref[0, at] = (grad * up * sg * (1.0 + gate * (1.0 - sg))).astype(bf16)
            out_ref[1, at] = (grad * silu).astype(bf16)
            out_ref[2, at] = (silu * up).astype(bf16)
            return carry

        lax.fori_loop(0, gate_s.shape[0] // chunk, body, 0)


def feed_forward_rows(second, cot, part, gate_up_weight, down_weight, tile=512):
    length, model = second.shape
    line, _, rows, _ = cot.shape
    hidden = down_weight.shape[0]
    return pl.pallas_call(
        rows_kernel,
        grid=(model // tile,),
        in_specs=[
            pl.BlockSpec((length, tile), lambda i: (0, i)),
            pl.BlockSpec((line, None, rows, tile), lambda i: (0, part, 0, i)),
            pl.BlockSpec((2, tile, hidden), lambda i: (0, i, 0)),
            pl.BlockSpec((hidden, tile), lambda i: (0, i)),
        ],
        out_specs=pl.BlockSpec((3, length, hidden), lambda i: (0, 0, 0), pipeline_mode=pl.Buffered(1)),
        out_shape=jax.ShapeDtypeStruct((3, length, hidden), bf16),
        scratch_shapes=[pltpu.VMEM((length, hidden), f32)] * 3,
        compiler_params=pltpu.CompilerParams(vmem_limit_bytes=56 * 1024 * 1024),
        cost_estimate=pl.CostEstimate(
            flops=6 * length * model * hidden, bytes_accessed=6 * model * hidden, transcendentals=length * hidden),
        name="feed_forward_rows",
    )(second, cot, gate_up_weight, down_weight)


def swap(value):
    return lax.ppermute(value, "core", [(0, 1), (1, 0)])


def planes_kernel(pieces, core_ref, *refs):
    out_ref, sent_ref = refs[2 * pieces:]
    lefts = [refs[p][...].T for p in range(pieces)]
    for s in range(out_ref.shape[0]):
        total = None
        for p in range(pieces):
            term = jnp.dot(lefts[p], refs[pieces + p][s], preferred_element_type=f32)
            total = term if total is None else total + term
        low = total.astype(bf16)
        sent_ref[s] = low
        out_ref[s] = low.astype(f32)


def planes_fill(core_ref, whole_ref, part_ref, out_ref):
    out_ref[...] = part_ref[...].astype(f32)


def planes_grad(core, lefts, rights, planes, tile=256):
    pieces = len(lefts)
    height = lefts[0].shape[1]
    _, depth, span = rights[0].shape
    steps = height // 2 // tile
    whole = jax.ShapeDtypeStruct((planes, height, span), f32)
    params = pltpu.CompilerParams(vmem_limit_bytes=48 * 1024 * 1024)
    own, sent = pl.pallas_call(
        functools.partial(planes_kernel, pieces),
        grid_spec=pltpu.PrefetchScalarGridSpec(
            num_scalar_prefetch=1,
            grid=(steps,),
            in_specs=[pl.BlockSpec((depth, tile), lambda i, c: (0, c[0] * steps + i))] * pieces
            + [pl.BlockSpec((planes, depth, span), lambda i, c: (0, 0, 0), pipeline_mode=pl.Buffered(1))] * pieces,
            out_specs=(
                pl.BlockSpec((planes, tile, span), lambda i, c: (0, c[0] * steps + i, 0)),
                pl.BlockSpec((planes, tile, span), lambda i, c: (0, i, 0)),
            ),
        ),
        out_shape=(whole, jax.ShapeDtypeStruct((planes, height // 2, span), bf16)),
        compiler_params=params,
        cost_estimate=pl.CostEstimate(
            flops=pieces * depth * planes * height * span // 4,
            bytes_accessed=planes * height * span, transcendentals=0),
        name="planes_grad",
    )(core, *lefts, *rights)

    def finish(part):
        return pl.pallas_call(
            planes_fill,
            grid_spec=pltpu.PrefetchScalarGridSpec(
                num_scalar_prefetch=1,
                grid=(planes, steps),
                in_specs=[
                    pl.BlockSpec(memory_space=pl.ANY),
                    pl.BlockSpec((1, tile, span), lambda s, i, c: (s, i, 0)),
                ],
                out_specs=pl.BlockSpec((1, tile, span), lambda s, i, c: (s, (1 - c[0]) * steps + i, 0)),
            ),
            out_shape=whole,
            input_output_aliases={1: 0},
            compiler_params=params,
            cost_estimate=pl.CostEstimate(
                flops=planes * height * span // 2, bytes_accessed=3 * planes * height * span, transcendentals=0),
            name="planes_fill",
        )(core, own, part)

    return sent, finish


def turned_kernel(pieces, core_ref, *refs):
    out_ref, sent_ref = refs[2 * pieces:2 * pieces + 2]
    turned = refs[2 * pieces + 2:]

    @pl.when(pl.program_id(0) == 0)
    def _():
        for p in range(pieces):
            turned[p][...] = refs[p][...].T

    total = None
    for p in range(pieces):
        right = refs[pieces + p][...]
        right = right.reshape(-1, right.shape[-1])
        term = jnp.dot(turned[p][...], right, preferred_element_type=f32)
        total = term if total is None else total + term
    low = total.astype(bf16)
    sent_ref[...] = low
    out_ref[...] = low.astype(f32)


def turned_grad(core, lefts, rights, tile=256):
    pieces = len(lefts)
    _, depth, height = lefts[0].shape
    line, parts, rows, span = rights[0].shape

    def right_spec(h):
        return pl.BlockSpec((line, None, rows, tile), lambda i, c: (0, h, 0, c[0] * steps + i))

    steps = span // 2 // tile
    whole = jax.ShapeDtypeStruct((height, span), f32)
    params = pltpu.CompilerParams(vmem_limit_bytes=48 * 1024 * 1024)
    own, sent = pl.pallas_call(
        functools.partial(turned_kernel, pieces),
        grid_spec=pltpu.PrefetchScalarGridSpec(
            num_scalar_prefetch=1,
            grid=(steps,),
            in_specs=[pl.BlockSpec((None, depth, height), lambda i, c: (2, 0, 0), pipeline_mode=pl.Buffered(1))] * pieces
            + [right_spec(p % parts) for p in range(pieces)],
            out_specs=(
                pl.BlockSpec((height, tile), lambda i, c: (0, c[0] * steps + i)),
                pl.BlockSpec((height, tile), lambda i, c: (0, i)),
            ),
            scratch_shapes=[pltpu.VMEM((height, depth), bf16)] * pieces,
        ),
        out_shape=(whole, jax.ShapeDtypeStruct((height, span // 2), bf16)),
        compiler_params=params,
        cost_estimate=pl.CostEstimate(
            flops=pieces * depth * height * span // 4,
            bytes_accessed=height * span, transcendentals=0),
        name="turned_grad",
    )(core, *lefts, *[right for right in rights for _ in range(parts)])

    def finish(part):
        return pl.pallas_call(
            planes_fill,
            grid_spec=pltpu.PrefetchScalarGridSpec(
                num_scalar_prefetch=1,
                grid=(steps,),
                in_specs=[
                    pl.BlockSpec(memory_space=pl.ANY),
                    pl.BlockSpec((height, tile), lambda i, c: (0, i)),
                ],
                out_specs=pl.BlockSpec((height, tile), lambda i, c: (0, (1 - c[0]) * steps + i)),
            ),
            out_shape=whole,
            input_output_aliases={1: 0},
            compiler_params=params,
            cost_estimate=pl.CostEstimate(
                flops=height * span // 2, bytes_accessed=3 * height * span, transcendentals=0),
            name="turned_fill",
        )(core, own, part)

    return sent, finish


def norm_rows(values, gain):
    return values * lax.rsqrt(jnp.mean(values * values, axis=-1, keepdims=True) + 1e-06) * gain


def norm_back(grad, values, gain):
    scale = lax.rsqrt(jnp.mean(values * values, axis=-1, keepdims=True) + 1e-06)
    unit = values * scale
    inner = grad * gain
    back = scale * (inner - unit * jnp.mean(inner * unit, axis=-1, keepdims=True))
    return back, jnp.sum(grad * unit, axis=0)


def dot(equation, left, right):
    return jnp.einsum(equation, left, right, preferred_element_type=f32)


def after(value, *others):
    return lax.optimization_barrier((value, *others))[0]


def per_device(shards, hidden_in, norm1_gain, qkv_weight, beta_weight, conv_weight, out_gain,
               out_weight, norm2_gain, gate_up_weight, down_weight, block_segments, cotangent):
    segments = block_segments[0]
    blocks = segments.shape[0]
    rows, model = hidden_in.shape
    length = rows * shards
    me = lax.axis_index("head")
    mine_z = lax.axis_index("z")

    half = shards // 2

    def exchange(parts):
        return [parts[0]] + [
            lax.ppermute(parts[k], "head", [(i, i ^ k) for i in range(shards)])
            for k in range(1, shards)
        ]

    def move(value, k):
        return lax.ppermute(value, "head", [(i, i ^ k) for i in range(shards)])

    def relay(pieces):
        far = []
        for k in range(half + 1, shards):
            via = k ^ half
            cut = pieces[0].shape[0] // 2
            far.append((move(pieces[half][:cut], via), move(pieces[via][cut:], half)))
        return far

    def gather_rows(own):
        return exchange([own] * shards)

    def scatter_sum(product):
        pieces = exchange([product[k * rows:(k + 1) * rows] for k in range(shards)])
        total = pieces[0].astype(f32)
        for piece in pieces[1:]:
            total = total + piece.astype(f32)
        return total

    keep = jnp.concatenate([jnp.zeros((1,), bool), segments[1:] == segments[:-1]])
    info = jnp.concatenate([me[None], keep]).astype(jnp.int32)
    taps = conv_weight.astype(f32).reshape(-1, conv_weight.shape[2])
    taps = jnp.pad(taps, ((0, 16 - taps.shape[0]), (0, 0)))
    gain = out_gain[None]

    core = lax.axis_index("core")
    hidden_parts = gather_rows(hidden_in)
    normed_all = jnp.concatenate(
        [norm_rows(part.astype(f32), norm1_gain).astype(bf16) for part in hidden_parts]
    )
    rows_in = hidden_in.astype(f32)
    hidden_line = lax.all_gather(hidden_in, "z", axis=0)
    line = hidden_line.shape[0]
    projected = dot("td,sde->ste", normed_all, qkv_weight)
    cot_all = jnp.concatenate([after(part, projected) for part in gather_rows(cotangent)])
    cot_line = lax.all_gather(cot_all, "z", axis=0)
    beta_logit = dot("td,dh->th", normed_all, beta_weight)
    mixer_low, *saved = mixer_forward(
        info, after(projected, cot_all), beta_logit, taps, gain, rows, shards, blocks
    )
    attn_rows = scatter_sum(after(dot("tc,cd->td", mixer_low, out_weight).astype(bf16), hidden_line))
    middle = rows_in + attn_rows
    second_low = norm_rows(middle, norm2_gain).astype(bf16)
    second_all = jnp.concatenate(gather_rows(second_low))
    second_line = lax.all_gather(after(second_low, cot_line), "z", axis=0)
    hidden_ready = after(hidden_line, second_all)
    hidden_near = [move(hidden_ready, k) for k in range(1, half + 1)]

    def feed_forward(second, cot):
        gate_up = dot("td,sdf->stf", second, gate_up_weight)
        sigmoid_gate = jax.nn.sigmoid(gate_up[0])
        silu_gate = gate_up[0] * sigmoid_gate
        hidden_low = (silu_gate * gate_up[1]).astype(bf16)
        hidden_grad = dot("td,fd->tf", cot, down_weight)
        gate_grad = hidden_grad * gate_up[1] * sigmoid_gate * (1.0 + gate_up[0] * (1.0 - sigmoid_gate))
        up_grad = hidden_grad * silu_gate
        return hidden_low, jnp.stack([gate_grad, up_grad]).astype(bf16)

    hidden_low, gate_up_low = feed_forward(second_all, cot_all)
    second_grad = scatter_sum(after(dot("stf,sdf->td", gate_up_low, gate_up_weight).astype(bf16), *hidden_near))
    ffn_product = dot("tf,fd->td", hidden_low, down_weight).astype(bf16)
    middle_part, norm2_gain_grad = norm_back(after(second_grad, cot_line, ffn_product), middle, norm2_gain)
    middle_grad = cotangent.astype(f32) + middle_part
    attn_grad_all = jnp.concatenate(gather_rows(middle_grad.astype(bf16)))
    mixer_in_grad = dot("td,cd->tc", attn_grad_all, out_weight)

    projected_low, beta_logit_grad, conv_grad, out_gain_grad = mixer_backward(
        info, mixer_in_grad, projected, beta_logit, taps, gain, saved, rows, shards, blocks
    )
    projected_line = lax.all_gather(projected_low, "z", axis=1, tiled=True)
    second_ready = after(second_line, projected_low)
    second_parts = [second_ready] + [move(second_ready, k) for k in range(1, half + 1)]
    beta_low = beta_logit_grad[:, :beta_weight.shape[1]].astype(bf16)
    first_product = dot("ste,sde->td", projected_low, qkv_weight) + dot("th,dh->td", beta_low, beta_weight)
    beta_grad = dot("td,th->dh", normed_all, beta_low)

    both = jnp.stack([first_product.astype(bf16), ffn_product]).reshape(2, shards, rows, model)

    out_partial = dot("tc,td->cd", mixer_low, attn_grad_all).astype(bf16)
    span = out_partial.shape[0] // 2
    out_half = lax.dynamic_slice_in_dim(out_partial, core * span, span).astype(f32)
    out_half = out_half + swap(lax.dynamic_slice_in_dim(out_partial, (1 - core) * span, span)).astype(f32)
    out_half = out_half.astype(bf16)

    cot_other = swap(cot_line)
    cot_line = cot_line.reshape(line, 2, half * rows, model)
    second_lines, line_rows, others = [], [], []
    second_far = relay(second_parts)
    hidden_near = [after(piece, second_parts[half]) for piece in hidden_near]
    hidden_far = relay([hidden_line, *hidden_near])

    def joined(pair):
        return jnp.concatenate([after(part, line_rows[0]) for part in pair])

    for h in range(2):
        pieces = second_parts[:half]
        if h == 1:
            pieces = [after(second_parts[half], line_rows[0], out_half)] + [joined(pair) for pair in second_far]
        piece = jnp.stack(pieces, 1).reshape(line * half * rows, model)
        if h == 0:
            piece = after(piece, both, cot_other, second_parts[half])
        else:
            piece = after(piece, *[part for pair in hidden_far for part in pair], *others)
        second_lines.append(piece)
        others.append(swap(piece))
        line_rows.append(feed_forward_rows(piece, cot_line, h, gate_up_weight, down_weight))
    out_every = lax.all_gather(after(out_half, line_rows[0]), "z", axis=0)
    hidden_every = jnp.stack([hidden_line, *hidden_near, *[joined(pair) for pair in hidden_far]])
    both_parts = after(both, line_rows[0])
    first_grad, ffn_rows = sum(
        piece.astype(f32) for piece in exchange([both_parts[:, k] for k in range(shards)])
    )
    row_others = [swap(part) for part in line_rows]
    down_part, down_finish = turned_grad(
        core[None], [after(line_rows[0], row_others[0], projected_line, first_grad, *others), line_rows[1], *row_others],
        [cot_line, cot_other.reshape(cot_line.shape)],
    )
    normed_every = norm_rows(hidden_every.astype(f32), norm1_gain).astype(bf16)
    normed_every = normed_every.transpose(1, 0, 2, 3).reshape(line * length, model)

    first_grad = after(first_grad, down_part)
    block_out = (middle + ffn_rows).astype(bf16)
    rows_part, norm1_gain_grad = norm_back(first_grad, rows_in, norm1_gain)
    input_grad = middle_grad + rows_part
    gains = jnp.concatenate([norm1_gain_grad, norm2_gain_grad, out_gain_grad[0]])
    small = jnp.concatenate([gains, beta_grad.T.reshape(-1), conv_grad[:12].reshape(-1)]).reshape(-1, 128)

    def total(value, axis, size):
        values = [value] + [
            lax.ppermute(value, axis, [(i, i ^ k) for i in range(size)]) for k in range(1, size)
        ]
        while len(values) > 1:
            values = [left + right for left, right in zip(values[::2], values[1::2])]
        return values[0]

    gate_up_part, gate_up_finish = planes_grad(
        core[None], [after(second_lines[0], normed_every, down_part), second_lines[1], *others],
        [*line_rows, *row_others], 2,
    )
    small = total(small, "core", 2)
    qkv_part, qkv_finish = planes_grad(
        core[None], [after(normed_every, small, gate_up_part), swap(normed_every)],
        [projected_line, swap(projected_line)], 3,
    )
    down_grad = down_finish(after(swap(down_part), qkv_part))
    gate_up_grad = gate_up_finish(after(swap(gate_up_part), down_grad))
    out_every = after(out_every, gate_up_grad)
    small = total(after(small, out_every), "z", line)
    small = small.reshape(-1)
    gain_size = gains.size
    gains = total(small[:gain_size].reshape(-1, 128), "head", shards).reshape(-1)
    out_rows = jnp.sum(out_every.astype(f32), axis=0).astype(bf16)
    out_other = swap(out_rows)
    out_grad = jnp.where(
        core == 0, jnp.concatenate([out_rows, out_other]), jnp.concatenate([out_other, out_rows])
    ).astype(f32)
    qkv_grad = qkv_finish(after(swap(qkv_part), gate_up_grad))
    beta_size = beta_grad.size
    beta_grad = small[gain_size:gain_size + beta_size].reshape(beta_grad.shape[::-1]).T
    conv_grad = small[gain_size + beta_size:].reshape(conv_weight.shape)
    return (
        block_out,
        input_grad,
        gains[:model],
        qkv_grad,
        beta_grad,
        conv_grad,
        gains[2 * model:],
        out_grad,
        gains[model:2 * model],
        gate_up_grad,
        down_grad,
    )


def solution(mesh):
    groups, shards = mesh.devices.shape
    split = Mesh(mesh.devices.reshape(groups // 2, 2, shards), ("z", "core", "head"))
    tokens = P(("z", "core", "head"), None)
    placed = (
        tokens,
        P(),
        P(None, None, "head"),
        P(None, "head"),
        P(None, None, "head"),
        P(),
        P("head", None),
        P(),
        P(None, None, "head"),
        P("head", None),
        P(("z", "core"), None),
        tokens,
    )
    return jax.shard_map(
        lambda *args: per_device(shards, *args),
        mesh=split,
        in_specs=placed,
        out_specs=(
            tokens,
            tokens,
            P(),
            P(None, None, "head"),
            P(None, "head"),
            P(None, None, "head"),
            P(),
            P("head", None),
            P(),
            P(None, None, "head"),
            P("head", None),
        ),
        check_vma=False,
    )
```

```python
import functools
import jax
import jax.numpy as jnp
from jax import lax
from jax.experimental import pallas as pl
from jax.experimental.pallas import tpu as pltpu
from jax.sharding import Mesh, PartitionSpec as P

f32 = jnp.float32
bf16 = jnp.bfloat16

DIMS = {"nn": (((1,), (0,)), ((), ())), "nt": (((1,), (1,)), ((), ())), "tn": (((0,), (0,)), ((), ()))}


def mm(left, right, form="nn"):
    return lax.dot_general(left.astype(bf16), right.astype(bf16), DIMS[form], preferred_element_type=f32)


def halves(value):
    high = value.astype(bf16)
    return high, (value - high.astype(f32)).astype(bf16)


def mm3(left, right, form="nn"):
    lh, ll = halves(left)
    rh, rl = halves(right)
    return mm(lh, rh, form) + (mm(lh, rl, form) + mm(ll, rh, form))


def sigmoid(value):
    return 1.0 / (1.0 + jnp.exp(-value))


def block_masks(length, size):
    row = lax.broadcasted_iota(jnp.int32, (length, length), 0)
    col = lax.broadcasted_iota(jnp.int32, (length, length), 1)
    same = (row ^ col) < size
    return (same & (row > col)), (same & (row >= col))


def keep_rows(info_ref, length, size):
    row = lax.broadcasted_iota(jnp.int32, (length, 1), 0)
    keep = jnp.zeros((length, 1), f32)
    for b in range(length // size):
        keep = jnp.where((row >= b * size) & (row < (b + 1) * size), info_ref[1 + b].astype(f32), keep)
    within = row & (size - 1)
    return [None] + [jnp.where(within >= shift, 1.0, keep) for shift in range(1, 4)]


def taken(ref, lead, me, rows, shards, cols):
    parts = []
    for j in range(shards):
        at = pl.ds(pl.multiple_of((me ^ j) * rows, rows), rows)
        parts.append(ref[lead + (at, cols)] if lead is not None else ref[at, cols])
    return jnp.concatenate(parts, 0)


def put(ref, lead, me, rows, shards, cols, value):
    for j in range(shards):
        at = pl.ds(pl.multiple_of((me ^ j) * rows, rows), rows)
        ref[lead + (at, cols)] = value[j * rows:(j + 1) * rows].astype(ref.dtype)


def forward_kernel(rows, shards, blocks, info_ref, proj_ref, logit_ref, taps_ref, gain_ref,
                   mixed_ref, conv_ref, o_ref, fresh_ref, state_ref, inv_ref,
                   q_s, k_s, u_s, w_s):
    length = rows * shards
    size = length // blocks
    heads = logit_ref.shape[1]
    width = proj_ref.shape[2] // heads
    me = info_ref[0]
    masks = keep_rows(info_ref, length, size)
    strict, inclusive = block_masks(length, size)
    logit = taken(logit_ref, (), me, rows, shards, slice(None))
    beta_all = sigmoid(logit)
    for h in range(heads):
        cols = slice(h * width, (h + 1) * width)
        beta = beta_all[:, h:h + 1]
        acts = []
        for s in range(3):
            x = taken(proj_ref, (s,), me, rows, shards, cols)
            z = x * taps_ref[4 * s:4 * s + 1, cols]
            for j in range(1, 4):
                z = z + pltpu.roll(x, j, 0) * (taps_ref[4 * s + j:4 * s + j + 1, cols] * masks[j])
            conv_ref[s, :, cols] = z
            acts.append(z * sigmoid(z))
        q0, k0, v = acts
        q = q0 * (lax.rsqrt(jnp.sum(q0 * q0, axis=-1, keepdims=True) + 1e-06) * width ** -0.5)
        k = k0 * lax.rsqrt(jnp.sum(k0 * k0, axis=-1, keepdims=True) + 1e-06)
        q_s[:, cols] = q
        k_s[:, cols] = k
        power = jnp.where(strict, mm3(k * -beta, k, "nt"), 0.0)
        inverse = power
        step = 1
        while 2 * step < size:
            power = mm3(power, power)
            inverse = inverse + power + mm3(inverse, power)
            step *= 2
        inv_ref[h] = inverse
        bk, bv = beta * k, beta * v
        w_s[:, cols] = bk + mm(inverse, bk)
        u_s[:, cols] = bv + mm(inverse, bv)
    states = [jnp.zeros((width, width), f32)] * heads
    for b in range(blocks):
        at = slice(b * size, (b + 1) * size)
        keep = info_ref[1 + b].astype(f32)
        for h in range(heads):
            cols = slice(h * width, (h + 1) * width)
            state = states[h] * keep
            state_ref[h, b] = state
            fresh = u_s[at, cols] - mm(w_s[at, cols], state)
            fresh_ref[at, cols] = fresh
            states[h] = state + mm(k_s[at, cols], fresh, "tn")
            o_ref[at, cols] = mm(q_s[at, cols], state)
    for h in range(heads):
        cols = slice(h * width, (h + 1) * width)
        scores = jnp.where(inclusive, mm(q_s[:, cols], k_s[:, cols], "nt"), 0.0)
        o = o_ref[:, cols] + mm(scores, fresh_ref[:, cols])
        o_ref[:, cols] = o
        mixed = o * lax.rsqrt(jnp.mean(o * o, axis=-1, keepdims=True) + 1e-05) * gain_ref[0:1, :]
        put(mixed_ref, (), me, rows, shards, cols, mixed)


def backward_kernel(rows, shards, blocks, info_ref, grad_ref, proj_ref, logit_ref, taps_ref, gain_ref,
                    conv_ref, o_ref, fresh_ref, state_ref, inv_ref,
                    proj_grad_ref, logit_grad_ref, taps_grad_ref, gain_grad_ref,
                    q_s, k_s, w_s, do_s, df_s, dq_s, dk_s):
    length = rows * shards
    size = length // blocks
    heads = logit_ref.shape[1]
    width = proj_ref.shape[2] // heads
    me = info_ref[0]
    masks = keep_rows(info_ref, length, size)
    strict, inclusive = block_masks(length, size)
    logit = taken(logit_ref, (), me, rows, shards, slice(None))
    beta_all = sigmoid(logit)
    gain_total = jnp.zeros((1, width), f32)
    lane = lax.broadcasted_iota(jnp.int32, (length, logit_grad_ref.shape[1]), 1)
    logit_grad = jnp.zeros((length, logit_grad_ref.shape[1]), f32)
    for h in range(heads):
        cols = slice(h * width, (h + 1) * width)
        beta = beta_all[:, h:h + 1]
        zq, zk = conv_ref[0, :, cols], conv_ref[1, :, cols]
        q0, k0 = zq * sigmoid(zq), zk * sigmoid(zk)
        q = q0 * (lax.rsqrt(jnp.sum(q0 * q0, axis=-1, keepdims=True) + 1e-06) * width ** -0.5)
        k = k0 * lax.rsqrt(jnp.sum(k0 * k0, axis=-1, keepdims=True) + 1e-06)
        q_s[:, cols] = q
        k_s[:, cols] = k
        bk = beta * k
        w_s[:, cols] = bk + mm(inv_ref[h], bk)
        g = taken(grad_ref, (), me, rows, shards, cols)
        o = o_ref[:, cols]
        r = lax.rsqrt(jnp.mean(o * o, axis=-1, keepdims=True) + 1e-05)
        on = o * r
        gain_total = gain_total + jnp.sum(g * on, axis=0, keepdims=True)
        dn = g * gain_ref[0:1, :]
        do = r * (dn - on * jnp.mean(dn * on, axis=-1, keepdims=True))
        do_s[:, cols] = do
        scores = jnp.where(inclusive, mm(q, k, "nt"), 0.0)
        df_s[:, cols] = mm(scores, do, "tn")
        dscores = jnp.where(inclusive, mm(do, fresh_ref[:, cols], "nt"), 0.0)
        dq_s[:, cols] = mm(dscores, k)
        dk_s[:, cols] = mm(dscores, q, "tn")
    gain_grad_ref[...] = jnp.broadcast_to(gain_total, gain_grad_ref.shape)
    carried = [jnp.zeros((width, width), f32)] * heads
    for b in reversed(range(blocks)):
        at = slice(b * size, (b + 1) * size)
        keep = info_ref[1 + b].astype(f32)
        for h in range(heads):
            cols = slice(h * width, (h + 1) * width)
            after = carried[h]
            df = df_s[at, cols] + mm(k_s[at, cols], after)
            df_s[at, cols] = df
            do = do_s[at, cols]
            carried[h] = keep * (after + mm(q_s[at, cols], do, "tn") - mm(w_s[at, cols], df, "tn"))
            dq_s[at, cols] = dq_s[at, cols] + mm(do, state_ref[h, b], "nt")
            dk_s[at, cols] = dk_s[at, cols] + mm(fresh_ref[at, cols], after, "nt")
    for h in range(heads):
        cols = slice(h * width, (h + 1) * width)
        beta = beta_all[:, h:h + 1]
        k = k_s[:, cols]
        df = df_s[:, cols]
        dr = df + mm(inv_ref[h], df, "tn")
        bdr = beta * dr
        fresh = fresh_ref[:, cols]
        lower = jnp.where(strict, mm(dr, fresh, "nt"), 0.0)
        blower = beta * lower
        zv = conv_ref[2, :, cols]
        sv = sigmoid(zv)
        held, back = [], []
        for b in range(blocks):
            at = slice(b * size, (b + 1) * size)
            held.append(mm(k[at], state_ref[h, b]))
            back.append(mm(bdr[at], state_ref[h, b], "nt"))
        excess = zv * sv - jnp.concatenate(held, 0)
        gram = mm(k, k, "nt")
        dbeta = jnp.sum(dr * excess, axis=-1, keepdims=True) - jnp.sum(lower * gram, axis=-1, keepdims=True)
        logit_grad = jnp.where(lane == h, dbeta * beta * (1.0 - beta), logit_grad)
        dk = dk_s[:, cols] - jnp.concatenate(back, 0) - (mm(blower, k) + mm(blower, k, "tn"))
        dq = dq_s[:, cols]
        for s, dy in ((0, dq), (1, dk), (2, bdr)):
            z = conv_ref[s, :, cols]
            sz = sigmoid(z)
            if s < 2:
                y = z * sz
                r = lax.rsqrt(jnp.sum(y * y, axis=-1, keepdims=True) + 1e-06)
                yn = y * r
                if s == 0:
                    r = r * width ** -0.5
                dy = r * (dy - yn * jnp.sum(dy * yn, axis=-1, keepdims=True))
            dz = dy * sz * (1.0 + z * (1.0 - sz))
            x = taken(proj_ref, (s,), me, rows, shards, cols)
            dx = dz * taps_ref[4 * s:4 * s + 1, cols]
            taps_grad_ref[4 * s:4 * s + 1, cols] = jnp.sum(dz * x, axis=0, keepdims=True)
            for j in range(1, 4):
                moved = dz * masks[j]
                taps_grad_ref[4 * s + j:4 * s + j + 1, cols] = jnp.sum(moved * pltpu.roll(x, j, 0), axis=0, keepdims=True)
                dx = dx + pltpu.roll(moved, length - j, 0) * taps_ref[4 * s + j:4 * s + j + 1, cols]
            put(proj_grad_ref, (s,), me, rows, shards, cols, dx)
    put(logit_grad_ref, (), me, rows, shards, slice(None), logit_grad)


SMEM = pl.BlockSpec(memory_space=pltpu.SMEM)
VMEM = pl.BlockSpec(memory_space=pltpu.VMEM)


def mixer_forward(info, projected, logit, taps, gain, rows, shards, blocks):
    _, length, span = projected.shape
    heads = logit.shape[1]
    width = span // heads
    shape = jax.ShapeDtypeStruct
    return pl.pallas_call(
        functools.partial(forward_kernel, rows, shards, blocks),
        out_shape=(
            shape((length, span), bf16),
            shape((3, length, span), f32),
            shape((length, span), f32),
            shape((length, span), f32),
            shape((heads, blocks, width, width), f32),
            shape((heads, length, length), f32),
        ),
        in_specs=[SMEM] + [VMEM] * 4,
        out_specs=(VMEM,) * 6,
        scratch_shapes=[pltpu.VMEM((length, span), f32)] * 4,
        compiler_params=pltpu.CompilerParams(vmem_limit_bytes=48 * 1024 * 1024),
        cost_estimate=pl.CostEstimate(flops=10**10, bytes_accessed=10 * 2**20, transcendentals=10**6),
        name="mixer_forward",
    )(info, projected, logit, taps, gain)


def mixer_backward(info, grad, projected, logit, taps, gain, saved, rows, shards, blocks):
    _, length, span = projected.shape
    heads = logit.shape[1]
    width = span // heads
    shape = jax.ShapeDtypeStruct
    return pl.pallas_call(
        functools.partial(backward_kernel, rows, shards, blocks),
        out_shape=(
            shape((3, length, span), bf16),
            shape((length, 128), f32),
            shape((16, span), f32),
            shape((8, width), f32),
        ),
        in_specs=[SMEM] + [VMEM] * 10,
        out_specs=(VMEM,) * 4,
        scratch_shapes=[pltpu.VMEM((length, span), f32)] * 7,
        compiler_params=pltpu.CompilerParams(vmem_limit_bytes=48 * 1024 * 1024),
        cost_estimate=pl.CostEstimate(flops=2 * 10**10, bytes_accessed=14 * 2**20, transcendentals=10**6),
        name="mixer_backward",
    )(info, grad, projected, logit, taps, gain, *saved)


def rows_kernel(second_ref, cot_ref, gate_up_ref, down_ref, out_ref, gate_s, up_s, grad_s):
    step = pl.program_id(0)
    second = second_ref[...]
    cot = cot_ref[...]
    cot = cot.reshape(-1, cot.shape[-1])
    gate = jnp.dot(second, gate_up_ref[0], preferred_element_type=f32)
    up = jnp.dot(second, gate_up_ref[1], preferred_element_type=f32)
    grad = lax.dot_general(cot, down_ref[...], DIMS["nt"], preferred_element_type=f32)

    @pl.when(step == 0)
    def _():
        gate_s[...] = gate
        up_s[...] = up
        grad_s[...] = grad

    @pl.when(step > 0)
    def _():
        gate_s[...] += gate
        up_s[...] += up
        grad_s[...] += grad

    @pl.when(step == pl.num_programs(0) - 1)
    def _():
        chunk = 32

        def body(r, carry):
            at = pl.ds(pl.multiple_of(r * chunk, chunk), chunk)
            gate, up, grad = gate_s[at], up_s[at], grad_s[at]
            sg = sigmoid(gate)
            silu = gate * sg
            out_ref[0, at] = (grad * up * sg * (1.0 + gate * (1.0 - sg))).astype(bf16)
            out_ref[1, at] = (grad * silu).astype(bf16)
            out_ref[2, at] = (silu * up).astype(bf16)
            return carry

        lax.fori_loop(0, gate_s.shape[0] // chunk, body, 0)


def feed_forward_rows(second, cot, part, gate_up_weight, down_weight, tile=512):
    length, model = second.shape
    line, _, rows, _ = cot.shape
    hidden = down_weight.shape[0]
    return pl.pallas_call(
        rows_kernel,
        grid=(model // tile,),
        in_specs=[
            pl.BlockSpec((length, tile), lambda i: (0, i)),
            pl.BlockSpec((line, None, rows, tile), lambda i: (0, part, 0, i)),
            pl.BlockSpec((2, tile, hidden), lambda i: (0, i, 0)),
            pl.BlockSpec((hidden, tile), lambda i: (0, i)),
        ],
        out_specs=pl.BlockSpec((3, length, hidden), lambda i: (0, 0, 0), pipeline_mode=pl.Buffered(1)),
        out_shape=jax.ShapeDtypeStruct((3, length, hidden), bf16),
        scratch_shapes=[pltpu.VMEM((length, hidden), f32)] * 3,
        compiler_params=pltpu.CompilerParams(vmem_limit_bytes=56 * 1024 * 1024),
        cost_estimate=pl.CostEstimate(
            flops=6 * length * model * hidden, bytes_accessed=6 * model * hidden, transcendentals=length * hidden),
        name="feed_forward_rows",
    )(second, cot, gate_up_weight, down_weight)


def swap(value):
    return lax.ppermute(value, "core", [(0, 1), (1, 0)])


def planes_kernel(pieces, core_ref, *refs):
    out_ref, sent_ref = refs[2 * pieces:]
    lefts = [refs[p][...].T for p in range(pieces)]
    for s in range(out_ref.shape[0]):
        total = None
        for p in range(pieces):
            term = jnp.dot(lefts[p], refs[pieces + p][s], preferred_element_type=f32)
            total = term if total is None else total + term
        low = total.astype(bf16)
        sent_ref[s] = low
        out_ref[s] = low.astype(f32)


def planes_fill(core_ref, whole_ref, part_ref, out_ref):
    out_ref[...] = part_ref[...].astype(f32)


def planes_grad(core, lefts, rights, planes, tile=256):
    pieces = len(lefts)
    height = lefts[0].shape[1]
    _, depth, span = rights[0].shape
    steps = height // 2 // tile
    whole = jax.ShapeDtypeStruct((planes, height, span), f32)
    params = pltpu.CompilerParams(vmem_limit_bytes=48 * 1024 * 1024)
    own, sent = pl.pallas_call(
        functools.partial(planes_kernel, pieces),
        grid_spec=pltpu.PrefetchScalarGridSpec(
            num_scalar_prefetch=1,
            grid=(steps,),
            in_specs=[pl.BlockSpec((depth, tile), lambda i, c: (0, c[0] * steps + i))] * pieces
            + [pl.BlockSpec((planes, depth, span), lambda i, c: (0, 0, 0), pipeline_mode=pl.Buffered(1))] * pieces,
            out_specs=(
                pl.BlockSpec((planes, tile, span), lambda i, c: (0, c[0] * steps + i, 0)),
                pl.BlockSpec((planes, tile, span), lambda i, c: (0, i, 0)),
            ),
        ),
        out_shape=(whole, jax.ShapeDtypeStruct((planes, height // 2, span), bf16)),
        compiler_params=params,
        cost_estimate=pl.CostEstimate(
            flops=pieces * depth * planes * height * span // 4,
            bytes_accessed=planes * height * span, transcendentals=0),
        name="planes_grad",
    )(core, *lefts, *rights)

    def finish(part):
        return pl.pallas_call(
            planes_fill,
            grid_spec=pltpu.PrefetchScalarGridSpec(
                num_scalar_prefetch=1,
                grid=(planes, steps),
                in_specs=[
                    pl.BlockSpec(memory_space=pl.ANY),
                    pl.BlockSpec((1, tile, span), lambda s, i, c: (s, i, 0)),
                ],
                out_specs=pl.BlockSpec((1, tile, span), lambda s, i, c: (s, (1 - c[0]) * steps + i, 0)),
            ),
            out_shape=whole,
            input_output_aliases={1: 0},
            compiler_params=params,
            cost_estimate=pl.CostEstimate(
                flops=planes * height * span // 2, bytes_accessed=3 * planes * height * span, transcendentals=0),
            name="planes_fill",
        )(core, own, part)

    return sent, finish


def turned_kernel(pieces, core_ref, *refs):
    out_ref, sent_ref = refs[2 * pieces:2 * pieces + 2]
    turned = refs[2 * pieces + 2:]

    @pl.when(pl.program_id(0) == 0)
    def _():
        for p in range(pieces):
            turned[p][...] = refs[p][...].T

    total = None
    for p in range(pieces):
        right = refs[pieces + p][...]
        right = right.reshape(-1, right.shape[-1])
        term = jnp.dot(turned[p][...], right, preferred_element_type=f32)
        total = term if total is None else total + term
    low = total.astype(bf16)
    sent_ref[...] = low
    out_ref[...] = low.astype(f32)


def turned_grad(core, lefts, rights, tile=256):
    pieces = len(lefts)
    _, depth, height = lefts[0].shape
    line, parts, rows, span = rights[0].shape

    def right_spec(h):
        return pl.BlockSpec((line, None, rows, tile), lambda i, c: (0, h, 0, c[0] * steps + i))

    steps = span // 2 // tile
    whole = jax.ShapeDtypeStruct((height, span), f32)
    params = pltpu.CompilerParams(vmem_limit_bytes=48 * 1024 * 1024)
    own, sent = pl.pallas_call(
        functools.partial(turned_kernel, pieces),
        grid_spec=pltpu.PrefetchScalarGridSpec(
            num_scalar_prefetch=1,
            grid=(steps,),
            in_specs=[pl.BlockSpec((None, depth, height), lambda i, c: (2, 0, 0), pipeline_mode=pl.Buffered(1))] * pieces
            + [right_spec(p % parts) for p in range(pieces)],
            out_specs=(
                pl.BlockSpec((height, tile), lambda i, c: (0, c[0] * steps + i)),
                pl.BlockSpec((height, tile), lambda i, c: (0, i)),
            ),
            scratch_shapes=[pltpu.VMEM((height, depth), bf16)] * pieces,
        ),
        out_shape=(whole, jax.ShapeDtypeStruct((height, span // 2), bf16)),
        compiler_params=params,
        cost_estimate=pl.CostEstimate(
            flops=pieces * depth * height * span // 4,
            bytes_accessed=height * span, transcendentals=0),
        name="turned_grad",
    )(core, *lefts, *[right for right in rights for _ in range(parts)])

    def finish(part):
        return pl.pallas_call(
            planes_fill,
            grid_spec=pltpu.PrefetchScalarGridSpec(
                num_scalar_prefetch=1,
                grid=(steps,),
                in_specs=[
                    pl.BlockSpec(memory_space=pl.ANY),
                    pl.BlockSpec((height, tile), lambda i, c: (0, i)),
                ],
                out_specs=pl.BlockSpec((height, tile), lambda i, c: (0, (1 - c[0]) * steps + i)),
            ),
            out_shape=whole,
            input_output_aliases={1: 0},
            compiler_params=params,
            cost_estimate=pl.CostEstimate(
                flops=height * span // 2, bytes_accessed=3 * height * span, transcendentals=0),
            name="turned_fill",
        )(core, own, part)

    return sent, finish


def norm_rows(values, gain):
    return values * lax.rsqrt(jnp.mean(values * values, axis=-1, keepdims=True) + 1e-06) * gain


def norm_back(grad, values, gain):
    scale = lax.rsqrt(jnp.mean(values * values, axis=-1, keepdims=True) + 1e-06)
    unit = values * scale
    inner = grad * gain
    back = scale * (inner - unit * jnp.mean(inner * unit, axis=-1, keepdims=True))
    return back, jnp.sum(grad * unit, axis=0)


def dot(equation, left, right):
    return jnp.einsum(equation, left, right, preferred_element_type=f32)


def after(value, *others):
    return lax.optimization_barrier((value, *others))[0]


def per_device(shards, hidden_in, norm1_gain, qkv_weight, beta_weight, conv_weight, out_gain,
               out_weight, norm2_gain, gate_up_weight, down_weight, block_segments, cotangent):
    segments = block_segments[0]
    blocks = segments.shape[0]
    rows, model = hidden_in.shape
    length = rows * shards
    me = lax.axis_index("head")
    mine_z = lax.axis_index("z")

    half = shards // 2

    def exchange(parts):
        return [parts[0]] + [
            lax.ppermute(parts[k], "head", [(i, i ^ k) for i in range(shards)])
            for k in range(1, shards)
        ]

    def move(value, k):
        return lax.ppermute(value, "head", [(i, i ^ k) for i in range(shards)])

    def relay(pieces):
        far = []
        for k in range(half + 1, shards):
            via = k ^ half
            cut = pieces[0].shape[0] // 2
            far.append((move(pieces[half][:cut], via), move(pieces[via][cut:], half)))
        return far

    def gather_rows(own):
        return exchange([own] * shards)

    def scatter_sum(product):
        pieces = exchange([product[k * rows:(k + 1) * rows] for k in range(shards)])
        total = pieces[0].astype(f32)
        for piece in pieces[1:]:
            total = total + piece.astype(f32)
        return total

    keep = jnp.concatenate([jnp.zeros((1,), bool), segments[1:] == segments[:-1]])
    info = jnp.concatenate([me[None], keep]).astype(jnp.int32)
    taps = conv_weight.astype(f32).reshape(-1, conv_weight.shape[2])
    taps = jnp.pad(taps, ((0, 16 - taps.shape[0]), (0, 0)))
    gain = out_gain[None]

    core = lax.axis_index("core")
    hidden_parts = gather_rows(hidden_in)
    normed_all = jnp.concatenate(
        [norm_rows(part.astype(f32), norm1_gain).astype(bf16) for part in hidden_parts]
    )
    rows_in = hidden_in.astype(f32)
    hidden_line = lax.all_gather(hidden_in, "z", axis=0)
    line = hidden_line.shape[0]
    projected = dot("td,sde->ste", normed_all, qkv_weight)
    cot_all = jnp.concatenate([after(part, projected) for part in gather_rows(cotangent)])
    cot_line = lax.all_gather(cot_all, "z", axis=0)
    beta_logit = dot("td,dh->th", normed_all, beta_weight)
    mixer_low, *saved = mixer_forward(
        info, after(projected, cot_all), beta_logit, taps, gain, rows, shards, blocks
    )
    attn_rows = scatter_sum(after(dot("tc,cd->td", mixer_low, out_weight).astype(bf16), hidden_line))
    middle = rows_in + attn_rows
    second_low = norm_rows(middle, norm2_gain).astype(bf16)
    second_all = jnp.concatenate(gather_rows(second_low))
    second_line = lax.all_gather(after(second_low, cot_line), "z", axis=0)
    hidden_ready = after(hidden_line, second_all)
    hidden_near = [move(hidden_ready, k) for k in range(1, half + 1)]

    def feed_forward(second, cot):
        gate_up = dot("td,sdf->stf", second, gate_up_weight)
        sigmoid_gate = jax.nn.sigmoid(gate_up[0])
        silu_gate = gate_up[0] * sigmoid_gate
        hidden_low = (silu_gate * gate_up[1]).astype(bf16)
        hidden_grad = dot("td,fd->tf", cot, down_weight)
        gate_grad = hidden_grad * gate_up[1] * sigmoid_gate * (1.0 + gate_up[0] * (1.0 - sigmoid_gate))
        up_grad = hidden_grad * silu_gate
        return hidden_low, jnp.stack([gate_grad, up_grad]).astype(bf16)

    hidden_low, gate_up_low = feed_forward(second_all, cot_all)
    second_grad = scatter_sum(after(dot("stf,sdf->td", gate_up_low, gate_up_weight).astype(bf16), *hidden_near))
    ffn_product = dot("tf,fd->td", hidden_low, down_weight).astype(bf16)
    middle_part, norm2_gain_grad = norm_back(after(second_grad, cot_line, ffn_product), middle, norm2_gain)
    middle_grad = cotangent.astype(f32) + middle_part
    attn_grad_all = jnp.concatenate(gather_rows(middle_grad.astype(bf16)))
    mixer_in_grad = dot("td,cd->tc", attn_grad_all, out_weight)

    projected_low, beta_logit_grad, conv_grad, out_gain_grad = mixer_backward(
        info, mixer_in_grad, projected, beta_logit, taps, gain, saved, rows, shards, blocks
    )
    projected_line = lax.all_gather(projected_low, "z", axis=1, tiled=True)
    second_ready = after(second_line, projected_low)
    second_parts = [second_ready] + [move(second_ready, k) for k in range(1, half + 1)]
    beta_low = beta_logit_grad[:, :beta_weight.shape[1]].astype(bf16)
    first_product = dot("ste,sde->td", projected_low, qkv_weight) + dot("th,dh->td", beta_low, beta_weight)
    beta_grad = dot("td,th->dh", normed_all, beta_low)

    both = jnp.stack([first_product.astype(bf16), ffn_product]).reshape(2, shards, rows, model)

    out_partial = dot("tc,td->cd", mixer_low, attn_grad_all).astype(bf16)
    span = out_partial.shape[0] // 2
    out_half = lax.dynamic_slice_in_dim(out_partial, core * span, span).astype(f32)
    out_half = out_half + swap(lax.dynamic_slice_in_dim(out_partial, (1 - core) * span, span)).astype(f32)
    out_half = out_half.astype(bf16)

    cot_other = swap(cot_line)
    cot_line = cot_line.reshape(line, 2, half * rows, model)
    second_lines, line_rows, others = [], [], []
    second_far = relay(second_parts)
    hidden_near = [after(piece, second_parts[half]) for piece in hidden_near]
    hidden_far = relay([hidden_line, *hidden_near])

    def joined(pair):
        return jnp.concatenate([after(part, line_rows[0]) for part in pair])

    for h in range(2):
        pieces = second_parts[:half]
        if h == 1:
            pieces = [after(second_parts[half], line_rows[0], out_half)] + [joined(pair) for pair in second_far]
        piece = jnp.stack(pieces, 1).reshape(line * half * rows, model)
        if h == 0:
            piece = after(piece, both, cot_other, second_parts[half])
        else:
            piece = after(piece, *[part for pair in hidden_far for part in pair], *others)
        second_lines.append(piece)
        others.append(swap(piece))
        line_rows.append(feed_forward_rows(piece, cot_line, h, gate_up_weight, down_weight))
    out_every = lax.all_gather(after(out_half, line_rows[0]), "z", axis=0)
    hidden_every = jnp.stack([hidden_line, *hidden_near, *[joined(pair) for pair in hidden_far]])
    both_parts = after(both, line_rows[0])
    first_grad, ffn_rows = sum(
        piece.astype(f32) for piece in exchange([both_parts[:, k] for k in range(shards)])
    )
    row_others = [swap(part) for part in line_rows]
    down_part, down_finish = turned_grad(
        core[None], [after(line_rows[0], row_others[0], projected_line, first_grad, *others), line_rows[1], *row_others],
        [cot_line, cot_other.reshape(cot_line.shape)],
    )
    normed_every = norm_rows(hidden_every.astype(f32), norm1_gain).astype(bf16)
    normed_every = normed_every.transpose(1, 0, 2, 3).reshape(line * length, model)

    first_grad = after(first_grad, down_part)
    block_out = (middle + ffn_rows).astype(bf16)
    rows_part, norm1_gain_grad = norm_back(first_grad, rows_in, norm1_gain)
    input_grad = middle_grad + rows_part
    gains = jnp.concatenate([norm1_gain_grad, norm2_gain_grad, out_gain_grad[0]])
    small = jnp.concatenate([gains, beta_grad.T.reshape(-1), conv_grad[:12].reshape(-1)]).reshape(-1, 128)

    def total(value, axis, size):
        values = [value] + [
            lax.ppermute(value, axis, [(i, i ^ k) for i in range(size)]) for k in range(1, size)
        ]
        while len(values) > 1:
            values = [left + right for left, right in zip(values[::2], values[1::2])]
        return values[0]

    gate_up_part, gate_up_finish = planes_grad(
        core[None], [after(second_lines[0], normed_every, down_part), second_lines[1], *others],
        [*line_rows, *row_others], 2,
    )
    small = total(small, "core", 2)
    qkv_part, qkv_finish = planes_grad(
        core[None], [after(normed_every, gate_up_part), swap(normed_every)],
        [projected_line, swap(projected_line)], 3,
    )
    down_grad = down_finish(after(swap(down_part), qkv_part))
    gate_up_grad = gate_up_finish(after(swap(gate_up_part), down_grad))
    out_every = after(out_every, gate_up_grad)
    small = total(after(small, out_every), "z", line)
    small = small.reshape(-1)
    gain_size = gains.size
    gains = total(small[:gain_size].reshape(-1, 128), "head", shards).reshape(-1)
    out_rows = jnp.sum(out_every.astype(f32), axis=0).astype(bf16)
    out_other = swap(out_rows)
    out_grad = jnp.where(
        core == 0, jnp.concatenate([out_rows, out_other]), jnp.concatenate([out_other, out_rows])
    ).astype(f32)
    qkv_grad = qkv_finish(after(swap(qkv_part), gate_up_grad))
    beta_size = beta_grad.size
    beta_grad = small[gain_size:gain_size + beta_size].reshape(beta_grad.shape[::-1]).T
    conv_grad = small[gain_size + beta_size:].reshape(conv_weight.shape)
    return (
        block_out,
        input_grad,
        gains[:model],
        qkv_grad,
        beta_grad,
        conv_grad,
        gains[2 * model:],
        out_grad,
        gains[model:2 * model],
        gate_up_grad,
        down_grad,
    )


def solution(mesh):
    groups, shards = mesh.devices.shape
    split = Mesh(mesh.devices.reshape(groups // 2, 2, shards), ("z", "core", "head"))
    tokens = P(("z", "core", "head"), None)
    placed = (
        tokens,
        P(),
        P(None, None, "head"),
        P(None, "head"),
        P(None, None, "head"),
        P(),
        P("head", None),
        P(),
        P(None, None, "head"),
        P("head", None),
        P(("z", "core"), None),
        tokens,
    )
    return jax.shard_map(
        lambda *args: per_device(shards, *args),
        mesh=split,
        in_specs=placed,
        out_specs=(
            tokens,
            tokens,
            P(),
            P(None, None, "head"),
            P(None, "head"),
            P(None, None, "head"),
            P(),
            P("head", None),
            P(),
            P(None, None, "head"),
            P("head", None),
        ),
        check_vma=False,
    )
```
